1024 devices in a mesh: qa: 32 (over z_lo, x), qb: 32 (over z_hi, y, core).
Axes of the slice: x: 4, y: 8, z: 16 (z_hi: 2, z_lo: 8; z = z_hi * 8 + z_lo), core: 2. Of those that a mesh axis runs over, the one named last changes fastest.
Arguments:
- amplitudes: bfloat16 [2, 32, 32, 4, 128, 128], P(None, 'qa', 'qb'), may hold values from -6 to 6
- layer_gates: bfloat16 [8, 2, 128, 128], replicated, may hold values from -0.375 to 0.375
- pauli_blocks: bfloat16 [4, 2, 128, 128], replicated, may hold values from -0.375 to 0.375
- flip_masks: int32 [4], replicated, may hold values from 0 to 127
- phase_masks: int32 [4], replicated, may hold values from 0 to 131071
Outputs:
- final_state: bfloat16 [2, 32, 32, 4, 128, 128], P(None, 'qa', 'qb')
- pauli_image: float32 [2, 32, 32, 4, 128, 128], P(None, 'qa', 'qb')
The draws below stay inside these ranges and needn't reach their ends.
All inputs are finite; a program needn't handle non-finite values.
Results may differ from the reference program's by a relative error of at most 0.014.
Values may be sent and summed in bfloat16 or wider, within the bound.
No kernel may reach another device: no remote copies, remote signals or barrier semaphores. Data moves between devices by JAX's collectives and lax.ppermute only.
A program may use at most 32 MiB of HBM per device.

```python
import jax
import jax.numpy as jnp
from jax import lax

GATE = 128
ROW_BLOCKS = 4
LAYERS = 8
TERMS = 4
NA = 32
NB = 32


def touch_ends(drawn, own_key, smallest, top_value):
    spot = [jax.random.randint(jax.random.fold_in(own_key, axis), (), 0, length) for axis, length in enumerate(drawn.shape)]
    longest = drawn.shape.index(max(drawn.shape))
    neighbour = spot[:longest] + [(spot[longest] + 1) % drawn.shape[longest]] + spot[longest + 1:]
    return drawn.at[tuple(spot)].set(smallest).at[tuple(neighbour)].set(top_value)


def levels(key, shape, cuts, least, largest):
    level, own = 1.0, jax.random.fold_in(key, 6)
    for position, shards_of in cuts:
        draws = jnp.exp(jax.random.uniform(jax.random.fold_in(own, position), (shards_of,), jnp.float32, least / len(cuts), largest / len(cuts)))
        level = level * jnp.repeat(draws, shape[position] // shards_of).reshape([-1 if axis == position else 1 for axis in range(len(shape))])
    return level


def gaussian(stream_key, dims, spread, bound, cuts=(), kind=jnp.bfloat16):
    factor_of = levels(stream_key, dims, cuts, -0.22, 0.18) if cuts else 1.0
    array = jax.random.normal(stream_key, dims, jnp.float32) * spread * factor_of
    return jnp.minimum(jnp.maximum(array, -bound), bound).astype(kind)


def setup_inputs(seed: int = 0) -> dict:
    keys = jax.random.split(jax.random.key(seed), 6)
    return {
        "amplitudes": gaussian(keys[0], (2, NA, NB, ROW_BLOCKS, GATE, GATE), 1.0, 6.0, ((1, 32), (2, 32))),
        "layer_gates": gaussian(keys[1], (LAYERS, 2, GATE, GATE), (2 * GATE) ** -0.5, 0.375),
        "pauli_blocks": gaussian(keys[2], (TERMS, 2, GATE, GATE), (2 * GATE) ** -0.5, 0.375),
        "flip_masks": touch_ends(jax.random.randint(keys[3], (TERMS,), 0, GATE), jax.random.fold_in(keys[3], 1), 0, GATE - 1).astype(jnp.int32),
        "phase_masks": touch_ends(jax.random.randint(keys[4], (TERMS,), 0, GATE * NA * NB), jax.random.fold_in(keys[4], 1), 0, (GATE * NA * NB) - 1).astype(jnp.int32),
    }


def column_apply(real_part, imag_part, matrix_real, matrix_imag):
    def product(operand, matrix):
        return jnp.einsum('...rj,ij->...ri', operand, matrix, precision=lax.Precision.HIGHEST)
    return (product(real_part, matrix_real) - product(imag_part, matrix_imag),
            product(real_part, matrix_imag) + product(imag_part, matrix_real))


def row_apply(real_part, imag_part, matrix_real, matrix_imag):
    def product(operand, matrix):
        return jnp.einsum('ir,...rc->...ic', matrix, operand, precision=lax.Precision.HIGHEST)
    return (product(real_part, matrix_real) - product(imag_part, matrix_imag),
            product(real_part, matrix_imag) + product(imag_part, matrix_real))


def regroup_columns(part):
    piece_width = GATE // NB
    moved = part.reshape(NA, NB, ROW_BLOCKS, GATE, NB, piece_width)
    return jnp.swapaxes(moved, 1, 4).reshape(NA, NB, ROW_BLOCKS, GATE, GATE)


def regroup_rows(part):
    piece_width = GATE // NA
    moved = part.reshape(NA, NB, ROW_BLOCKS, NA, piece_width, GATE)
    return jnp.swapaxes(moved, 0, 3).reshape(NA, NB, ROW_BLOCKS, GATE, GATE)


def round_trip(part):
    rounded = lax.optimization_barrier(part.astype(jnp.bfloat16))
    return rounded.astype(jnp.float32)


def flip_bit(part, axis_pos, half_span):
    full_shape = part.shape
    count = full_shape[axis_pos]
    split_shape = full_shape[:axis_pos] + (count // (2 * half_span), 2, half_span) + full_shape[axis_pos + 1:]
    return jnp.flip(part.reshape(split_shape), axis_pos + 1).reshape(full_shape)


def bit_parity(value):
    folded = jnp.bitwise_xor(value, jnp.right_shift(value, 16))
    folded = jnp.bitwise_xor(folded, jnp.right_shift(folded, 8))
    folded = jnp.bitwise_xor(folded, jnp.right_shift(folded, 4))
    folded = jnp.bitwise_xor(folded, jnp.right_shift(folded, 2))
    folded = jnp.bitwise_xor(folded, jnp.right_shift(folded, 1))
    return jnp.bitwise_and(folded, 1)


def reference(amplitudes, layer_gates, pauli_blocks, flip_masks, phase_masks):
    real_part = amplitudes[0].astype(jnp.float32)
    imag_part = amplitudes[1].astype(jnp.float32)
    gates_wide = layer_gates.astype(jnp.float32)
    for layer_idx in range(LAYERS):
        if layer_idx % 2 == 0:
            real_part, imag_part = column_apply(regroup_columns(real_part), regroup_columns(imag_part),
                                                gates_wide[layer_idx, 0], gates_wide[layer_idx, 1])
        else:
            real_part, imag_part = row_apply(regroup_rows(real_part), regroup_rows(imag_part),
                                             gates_wide[layer_idx, 0], gates_wide[layer_idx, 1])
        real_part = round_trip(real_part)
        imag_part = round_trip(imag_part)
    final_state = jnp.stack([real_part, imag_part]).astype(jnp.bfloat16)
    blocks_wide = pauli_blocks.astype(jnp.float32)
    columns = jnp.arange(GATE, dtype=jnp.int32)
    device_id = (jnp.arange(NA, dtype=jnp.int32)[:, None] * NB + jnp.arange(NB, dtype=jnp.int32)[None, :])
    global_index = device_id[:, :, None] * GATE + columns[None, None, :]
    partner_moves = [(0, NA // 2), (1, NB // 2), (0, 1), (1, 1)]
    accum_real = jnp.zeros_like(real_part)
    accum_imag = jnp.zeros_like(imag_part)
    for term_idx in range(TERMS):
        axis_pos, half_span = partner_moves[term_idx]
        other_real = flip_bit(real_part, axis_pos, half_span)
        other_imag = flip_bit(imag_part, axis_pos, half_span)
        source_cols = jnp.bitwise_xor(columns, flip_masks[term_idx]).astype(jnp.int32)
        other_real = jnp.take(other_real, source_cols, axis=-1)
        other_imag = jnp.take(other_imag, source_cols, axis=-1)
        term_real, term_imag = column_apply(other_real, other_imag, blocks_wide[term_idx, 0], blocks_wide[term_idx, 1])
        parity = bit_parity(jnp.bitwise_and(global_index, phase_masks[term_idx]))
        sign_vector = (1 - 2 * parity).astype(jnp.float32)[:, :, None, None, :]
        accum_real = accum_real + sign_vector * term_real
        accum_imag = accum_imag + sign_vector * term_imag
    return final_state, jnp.stack([accum_real, accum_imag])
```

```python
import jax
import jax.numpy as jnp
from jax import lax
from jax.sharding import Mesh, PartitionSpec as P

FINE = ("zl2", "zl", "x1", "x0", "zh", "y", "c")
FINE_SIZES = (2, 4, 2, 2, 2, 8, 2)
BF = jnp.bfloat16
F32 = jnp.float32


def exchange(value, axes):
    return lax.all_to_all(value, axes, split_axis=0, concat_axis=0, tiled=True)


def parity_sign(value):
    for shift in (16, 8, 4, 2, 1):
        value = jnp.bitwise_xor(value, jnp.right_shift(value, shift))
    return (1 - 2 * jnp.bitwise_and(value, 1)).astype(F32)


def cgate(gates, idx):
    g = gates[idx]
    return jnp.concatenate(
        [jnp.concatenate([g[0], -g[1]], 1), jnp.concatenate([g[1], g[0]], 1)], 0
    )


def pre(amplitudes):
    x = amplitudes.reshape(2, 4, 128, 16, 8)
    return x.transpose(1, 3, 0, 4, 2).reshape(64, 16, 128)


def row_phase(r1, gates):
    x = r1.reshape(2, 32, 2, 8, 32, 4)
    x = x.transpose(2, 1, 5, 4, 0, 3)
    for half in range(2):
        v = cgate(gates, 1 + 4 * half)
        x = jnp.dot(v, x.reshape(256, 512), preferred_element_type=F32).astype(BF)
        x = x.reshape(2, 32, 4, 32, 16).transpose(0, 3, 2, 1, 4)
        v = cgate(gates, 3 + 4 * half)
        x = jnp.dot(v, x.reshape(256, 512), preferred_element_type=F32).astype(BF)
        if half == 0:
            x = x.reshape(2, 32, 4, 32, 16).transpose(0, 3, 2, 1, 4)
    x = x.reshape(2, 32, 4, 2, 8, 2, 2, 8)
    return x.transpose(4, 1, 3, 5, 2, 6, 7, 0).reshape(256, 4, 128)


def col_phase(r2, gates, blocks, flips, masks, a_mid):
    x = r2.reshape(16, 16, 2, 2, 4, 2, 8, 2)
    x = x.reshape(16, 16, 2, 2, 4, 2, 2, 4, 2)
    x = x.transpose(2, 3, 4, 0, 6, 8, 5, 1, 7)
    for half in range(2):
        v = cgate(gates, 4 * half)
        x = jnp.einsum("rj,ij->ri", x.reshape(512, 256), v, preferred_element_type=F32).astype(BF)
        x = x.reshape(16, 32, 2, 32, 4).transpose(0, 3, 2, 1, 4)
        v = cgate(gates, 2 + 4 * half)
        x = jnp.einsum("rj,ij->ri", x.reshape(512, 256), v, preferred_element_type=F32).astype(BF)
        if half == 0:
            x = x.reshape(16, 32, 2, 32, 4).transpose(0, 3, 2, 1, 4)
    f = x.reshape(2, 2, 4, 2, 16, 256)
    cols = jnp.arange(128, dtype=jnp.int32)
    a4 = jnp.arange(2, dtype=jnp.int32)
    arow = a4[:, None] * 16 + a_mid + a4[None, :]
    brow = jnp.arange(32, dtype=jnp.int32).reshape(2, 16)
    grow = (arow[:, :, None, None] * 32 + brow) * 128
    image = 0.0
    for k in range(4):
        if k == 0:
            g = f[::-1]
        elif k == 1:
            g = f[:, :, :, ::-1]
        elif k == 2:
            g = f[:, ::-1]
        else:
            g = f.reshape(2, 2, 4, 2, 8, 2, 256)[:, :, :, :, :, ::-1].reshape(f.shape)
        onehot = (cols[:, None] == jnp.bitwise_xor(cols, flips[k])[None, :]).astype(BF)
        blk = jnp.einsum("pij,jc->pic", blocks[k], onehot, preferred_element_type=F32)
        sc = parity_sign(jnp.bitwise_and(cols, masks[k]))
        blk = (blk * sc[:, None]).astype(BF)
        srow = parity_sign(jnp.bitwise_and(grow, masks[k])).astype(BF)
        g = g * srow[:, :, None, :, :, None]
        v = cgate(blk[None], 0)
        image = image + jnp.einsum("rj,ij->ri", g.reshape(512, 256), v, preferred_element_type=F32)

    def outgoing(val):
        val = val.reshape(2, 2, 4, 2, 16, 2, 128)
        return val.transpose(3, 0, 1, 4, 5, 2, 6).reshape(128, 8, 128)

    return outgoing(f), outgoing(image.astype(BF))


def post(r3):
    x = r3.reshape(4, 32, 2, 4, 128)
    return x.transpose(2, 0, 1, 3, 4).reshape(2, 1, 1, 4, 128, 128)


E1 = ("zh", "zl2", "zl", "x1", "x0")
E2 = ("zl", "x1", "x0", "y", "c")
E3 = ("zh", "zl2", "x0", "y", "c")


def local(amplitudes, layer_gates, pauli_blocks, flip_masks, phase_masks):
    a_mid = lax.axis_index("zl") * 4 + lax.axis_index("x1") * 2
    r1 = exchange(pre(amplitudes), E1)
    r2 = exchange(row_phase(r1, layer_gates), E2)
    f, im = col_phase(r2, layer_gates, pauli_blocks, flip_masks, phase_masks, a_mid)
    both = exchange(jnp.concatenate([f, im], axis=1), E3)
    return post(both[:, :8]), post(both[:, 8:]).astype(F32)


def solution(mesh):
    fine = Mesh(mesh.devices.reshape(FINE_SIZES), FINE)
    spec = P(None, ("zl2", "zl", "x1", "x0"), ("zh", "y", "c"), None, None, None)
    return jax.shard_map(
        local,
        mesh=fine,
        in_specs=(spec, P(), P(), P(), P()),
        out_specs=(spec, spec),
        check_vma=False,
    )
```

```python
import jax
import jax.numpy as jnp
import numpy as np
from jax import lax
from jax.experimental import pallas as pl
from jax.experimental.pallas import tpu as pltpu
from jax.sharding import Mesh, PartitionSpec as P

FINE = ("zl2", "zl", "x1", "x0", "zh", "y", "c")
FINE_SIZES = (2, 4, 2, 2, 2, 8, 2)
E1 = ("zh", "zl2", "zl", "x1", "x0")
E2 = ("zl", "x1", "x0", "y", "c")
E3 = ("zh", "zl2", "x0", "y", "c")
BF = jnp.bfloat16
F32 = jnp.float32
NT = (((1,), (1,)), ((), ()))
NN = (((1,), (0,)), ((), ()))


def exchange(value, axes):
    return lax.all_to_all(value, axes, split_axis=0, concat_axis=0, tiled=True)


def parity_sign(value):
    for shift in (16, 8, 4, 2, 1):
        value = jnp.bitwise_xor(value, jnp.right_shift(value, shift))
    return (1 - 2 * jnp.bitwise_and(value, 1)).astype(F32)


def reorder(sizes, perm):
    source = np.arange(int(np.prod(sizes))).reshape(sizes).transpose(perm).reshape(-1)
    return (source[:, None] == np.arange(source.size)[None, :]).astype(np.float32)


def dot(a, b, dims):
    return lax.dot_general(a, b, dims, preferred_element_type=F32)


def swap_pair(x0, x1, shift, lane):
    low = jnp.bitwise_and(lane, shift) == 0
    return (
        jnp.where(low, x0, pltpu.roll(x1, shift, 1)),
        jnp.where(low, pltpu.roll(x0, 128 - shift, 1), x1),
    )


def swap_quads(t, hi, lo, lane):
    a0, a2 = swap_pair(t[0], t[2], hi, lane)
    a1, a3 = swap_pair(t[1], t[3], hi, lane)
    b0, b1 = swap_pair(a0, a1, lo, lane)
    b2, b3 = swap_pair(a2, a3, lo, lane)
    return b0, b1, b2, b3


def lanes_of(rows):
    return lax.broadcasted_iota(jnp.int32, (rows, 128), 1)


def regroup(d_ref, q_ref, hi, lo):
    lane = lanes_of(32)
    for p in range(2):
        for g in range(4):
            t = [d_ref[pl.ds(p * 128 + i * 32, 32), pl.ds(g * 128, 128)] for i in range(4)]
            for s, block in enumerate(swap_quads(t, hi, lo, lane)):
                q_ref[pl.ds(g * 128 + s * 32, 32), pl.ds(p * 128, 128)] = block.astype(BF)


def pre_kernel(amp_ref, pr_ref, pc_ref, pm_ref, out_ref, z_ref):
    lane = lanes_of(32)
    for e in range(4):
        for p in range(2):
            turned = dot(pr_ref[...], amp_ref[p, e], NN).astype(BF)
            y = dot(pc_ref[...], turned, NT)
            t = [y[i * 32 : (i + 1) * 32] for i in range(4)]
            for i, block in enumerate(swap_quads(t, 64, 32, lane)):
                z_ref[pl.ds(p * 128 + i * 32, 32), pl.ds(e * 128, 128)] = block.astype(BF)
    moved = dot(pm_ref[...], z_ref[...], NN).astype(BF)
    for e in range(4):
        out_ref[pl.ds(e * 256, 256), :] = moved[:, e * 128 : (e + 1) * 128]


PR = reorder((32, 4), (1, 0))
PC = reorder((16, 2, 4), (2, 0, 1))
PM1 = reorder((2, 4, 16, 2), (2, 3, 0, 1))


def pre(amplitudes):
    out = pl.pallas_call(
        pre_kernel,
        out_shape=jax.ShapeDtypeStruct((1024, 128), BF),
        scratch_shapes=[pltpu.VMEM((256, 512), BF)],
        name="pre",
    )(amplitudes.reshape(2, 4, 128, 128), jnp.asarray(PR, BF), jnp.asarray(PC, BF), jnp.asarray(PM1, BF))
    return out.reshape(64, 16, 128)


def row_kernel(r_ref, v_ref, out_ref, x_ref, d_ref, q_ref):
    for b4 in range(2):
        x = r_ref[pl.ds(b4 * 512, 512), :].astype(F32).reshape(32, 2, 8, 128)
        for c1 in range(2):
            x_ref[:, pl.ds((b4 * 2 + c1) * 128, 128)] = x[:, c1].reshape(256, 128).astype(BF)
    d_ref[...] = dot(v_ref[0], x_ref[...], NN)
    regroup(d_ref, q_ref, 64, 32)
    d_ref[...] = dot(v_ref[1], q_ref[...], NT)
    regroup(d_ref, q_ref, 64, 32)
    d_ref[...] = dot(v_ref[2], q_ref[...], NT)
    regroup(d_ref, q_ref, 64, 32)
    d_ref[...] = dot(v_ref[3], q_ref[...], NT)
    lane = lanes_of(32)
    for piece in range(4):
        x = {}
        for p in range(2):
            for g in range(4):
                x[g >> 1, g & 1, p] = d_ref[pl.ds(p * 128 + piece * 32, 32), pl.ds(g * 128, 128)]
        for c1 in range(2):
            for p in range(2):
                x[0, c1, p], x[1, c1, p] = swap_pair(x[0, c1, p], x[1, c1, p], 8, lane)
        for b in range(2):
            for p in range(2):
                x[b, 0, p], x[b, 1, p] = swap_pair(x[b, 0, p], x[b, 1, p], 4, lane)
        for b in range(2):
            for c1 in range(2):
                x[b, c1, 0], x[b, c1, 1] = swap_pair(x[b, c1, 0], x[b, c1, 1], 2, lane)
        for (i, j, k), block in x.items():
            out_ref[pl.ds((i * 4 + j * 2 + k) * 128 + piece * 32, 32), :] = block.astype(BF)


def row_phase(r1, row):
    out = pl.pallas_call(
        row_kernel,
        out_shape=jax.ShapeDtypeStruct((1024, 128), BF),
        scratch_shapes=[pltpu.VMEM((256, 512), BF), pltpu.VMEM((256, 512), F32), pltpu.VMEM((512, 256), BF)],
        name="rows",
    )(r1.reshape(1024, 128), row)
    return out.reshape(256, 4, 128)


def col_kernel(r_ref, v_ref, w_ref, s_ref, pm_ref, out_ref, d_ref, q_ref, f_ref, z_ref):
    lane = lanes_of(8)
    sub = lax.broadcasted_iota(jnp.int32, (8, 128), 0)
    high = jnp.bitwise_and(lane, 4) != 0
    keep = (jnp.bitwise_and(sub, 4) != 0) == high
    for kk in range(8):
        halves = []
        for k in (2 * kk, 2 * kk + 1):
            block = r_ref[pl.ds(k * 64, 64), :].astype(F32)
            x = {}
            for i in range(8):
                tile = block[i * 8 : (i + 1) * 8]
                turned = pltpu.roll(tile, 4, 0)
                other = jnp.where(high, pltpu.roll(turned, 4, 1), pltpu.roll(turned, 124, 1))
                x[i >> 2, (i >> 1) & 1, i & 1] = jnp.where(keep, tile, other)
            for i in range(2):
                for j in range(2):
                    x[0, i, j], x[1, i, j] = swap_pair(x[0, i, j], x[1, i, j], 16, lane)
            for i in range(2):
                for j in range(2):
                    x[i, 0, j], x[i, 1, j] = swap_pair(x[i, 0, j], x[i, 1, j], 2, lane)
            for i in range(2):
                for j in range(2):
                    x[i, j, 0], x[i, j, 1] = swap_pair(x[i, j, 0], x[i, j, 1], 1, lane)
            halves.append(x)
        for a4 in range(2):
            for p in range(2):
                for a0 in range(2):
                    both = jnp.concatenate([h[a4, p, a0] for h in halves], 0).astype(BF)
                    q_ref[pl.ds((a4 * 2 + a0) * 128 + kk * 16, 16), pl.ds(p * 128, 128)] = both
    d_ref[...] = dot(v_ref[0], q_ref[...], NT)
    regroup(d_ref, q_ref, 2, 1)
    d_ref[...] = dot(v_ref[1], q_ref[...], NT)
    regroup(d_ref, q_ref, 64, 32)
    d_ref[...] = dot(v_ref[2], q_ref[...], NT)
    regroup(d_ref, q_ref, 64, 32)
    state = dot(q_ref[...], v_ref[3], NN).astype(BF)
    f_ref[...] = state
    for g in range(4):
        for p in range(2):
            z_ref[pl.ds(p * 128, 128), pl.ds(g * 128, 128)] = f_ref[pl.ds(g * 128, 128), pl.ds(p * 128, 128)]
    moved = dot(pm_ref[...], z_ref[...], NN).astype(F32)
    for b4 in range(2):
        for g in range(4):
            part = moved[b4 * 128 : (b4 + 1) * 128, g * 128 : (g + 1) * 128].reshape(16, 8, 128)
            out_ref[b4, g, :, 0] = part.astype(BF)
    rows = f_ref[...].astype(F32)
    flips = (
        jnp.concatenate([rows[256:], rows[:256]], 0),
        swap_rows(rows, 16),
        swap_rows(rows, 128),
        swap_rows(rows, 8),
    )
    image = None
    for k in range(4):
        signed = (flips[k] * jnp.concatenate([s_ref[k], s_ref[k]], 1).astype(F32)).astype(BF)
        term = dot(signed, w_ref[k], NT)
        image = term if image is None else image + term
    image = image.astype(BF)
    for g in range(4):
        for p in range(2):
            z_ref[pl.ds(p * 128, 128), pl.ds(g * 128, 128)] = image[g * 128 : (g + 1) * 128, p * 128 : (p + 1) * 128]
    moved = dot(pm_ref[...], z_ref[...], NN)
    for b4 in range(2):
        for g in range(4):
            part = moved[b4 * 128 : (b4 + 1) * 128, g * 128 : (g + 1) * 128].reshape(16, 8, 128)
            out_ref[b4, g, :, 1] = part.astype(BF)


def swap_rows(rows, half):
    n = rows.shape[0] // (2 * half)
    r = rows.reshape(n, 2, half, rows.shape[1])
    return jnp.concatenate([r[:, 1:], r[:, :1]], 1).reshape(rows.shape)


PM2 = reorder((2, 4, 2, 2, 8), (2, 4, 3, 0, 1))


def col_phase(r2, col, image, signs):
    out = pl.pallas_call(
        col_kernel,
        out_shape=jax.ShapeDtypeStruct((2, 4, 16, 2, 8, 128), BF),
        scratch_shapes=[
            pltpu.VMEM((256, 512), F32),
            pltpu.VMEM((512, 256), BF),
            pltpu.VMEM((512, 256), BF),
            pltpu.VMEM((256, 512), BF),
        ],
        name="cols",
    )(r2.reshape(1024, 128), col, image, signs, jnp.asarray(PM2, BF))
    return out.reshape(128, 16, 128)


def post_kernel(r_ref, pm_ref, f_ref, i_ref):
    for e in range(4):
        x = r_ref[pl.ds(e * 512, 512), :].astype(F32).reshape(32, 2, 8, 128)
        x = jnp.concatenate([x[:, h].reshape(256, 128) for h in range(2)], 1).astype(BF)
        moved = dot(pm_ref[...], x, NN)
        for p in range(2):
            f_ref[p, e] = moved[p * 128 : (p + 1) * 128, :128].astype(BF)
            i_ref[p, e] = moved[p * 128 : (p + 1) * 128, 128:]


PM3 = reorder((32, 2, 4), (1, 0, 2))


def post(r3):
    f, i = pl.pallas_call(
        post_kernel,
        out_shape=(jax.ShapeDtypeStruct((2, 4, 128, 128), BF), jax.ShapeDtypeStruct((2, 4, 128, 128), F32)),
        name="post",
    )(r3.reshape(2048, 128), jnp.asarray(PM3, BF))
    return f.reshape(2, 1, 1, 4, 128, 128), i.reshape(2, 1, 1, 4, 128, 128)


PT = reorder((2, 32, 4), (0, 2, 1))
C1 = reorder((2, 32, 4), (1, 0, 2))
C0 = reorder((2, 2, 2, 2, 2, 2, 4), (0, 6, 2, 1, 5, 3, 4))
R4 = reorder((2, 2, 8, 2, 4), (0, 4, 1, 3, 2))


def prep_kernel(flip_ref, mask_ref, mid_ref, g_ref, b_ref, p_ref, row_ref, col_ref, image_ref, sign_ref):
    pt = p_ref[0]

    def whole(real, imag):
        return jnp.concatenate(
            [jnp.concatenate([real, -imag], 1), jnp.concatenate([imag, real], 1)], 0
        )

    def moved(idx, left, right):
        v = whole(g_ref[idx, 0], g_ref[idx, 1])
        if left is not None:
            v = dot(left, v, NN).astype(BF)
        if right is not None:
            v = dot(v, right, NT).astype(BF)
        return v

    row_ref[0] = moved(1, pt, p_ref[1])
    row_ref[1] = moved(3, pt, pt)
    row_ref[2] = moved(5, pt, pt)
    row_ref[3] = moved(7, None, pt)
    col_ref[0] = moved(0, pt, p_ref[2])
    col_ref[1] = moved(2, pt, None)
    col_ref[2] = moved(4, p_ref[3], pt)
    col_ref[3] = dot(pt, whole(g_ref[6, 0], g_ref[6, 1]), NT).astype(BF)
    out_col = lax.broadcasted_iota(jnp.int32, (128, 128), 0)
    in_col = lax.broadcasted_iota(jnp.int32, (128, 128), 1)
    spot = lax.broadcasted_iota(jnp.int32, (512, 128), 0)
    o = jnp.bitwise_and(spot, 31)
    b = jnp.bitwise_and(o, 16) + jnp.bitwise_and(o, 7) * 2 + jnp.bitwise_and(jnp.right_shift(o, 3), 1)
    a = jnp.right_shift(spot, 8) * 16 + jnp.bitwise_and(jnp.right_shift(spot, 7), 1) + mid_ref[0]
    index = (a * 32 + b) * 128
    for k in range(4):
        onehot = (out_col == jnp.bitwise_xor(in_col, flip_ref[k])).astype(F32).astype(BF)
        sign = parity_sign(jnp.bitwise_and(out_col, mask_ref[k]))
        parts = [(dot(b_ref[k, q], onehot, NN) * sign).astype(BF) for q in range(2)]
        image_ref[k] = whole(parts[0], parts[1])
        sign_ref[k] = parity_sign(jnp.bitwise_and(index, mask_ref[k])).astype(BF)


def prep(gates, blocks, flips, masks, a_mid):
    smem = pl.BlockSpec(memory_space=pltpu.SMEM)
    vmem = pl.BlockSpec(memory_space=pltpu.VMEM)
    square = jax.ShapeDtypeStruct((4, 256, 256), BF)
    return pl.pallas_call(
        prep_kernel,
        in_specs=[smem, smem, smem, vmem, vmem, vmem],
        out_shape=(square, square, square, jax.ShapeDtypeStruct((4, 512, 128), BF)),
        name="prep",
    )(flips, masks, a_mid.reshape(1).astype(jnp.int32), gates, blocks, jnp.asarray(np.stack([PT, C1, C0, R4]), BF))


def local(amplitudes, layer_gates, pauli_blocks, flip_masks, phase_masks):
    a_mid = lax.axis_index("zl") * 4 + lax.axis_index("x1") * 2
    row, col, image, signs = prep(layer_gates, pauli_blocks, flip_masks, phase_masks, a_mid)
    r1 = exchange(pre(amplitudes), E1)
    r2 = exchange(row_phase(r1, row), E2)
    r3 = exchange(col_phase(r2, col, image, signs), E3)
    return post(r3)


def solution(mesh):
    fine = Mesh(mesh.devices.reshape(FINE_SIZES), FINE)
    spec = P(None, ("zl2", "zl", "x1", "x0"), ("zh", "y", "c"), None, None, None)
    return jax.shard_map(
        local,
        mesh=fine,
        in_specs=(spec, P(), P(), P(), P()),
        out_specs=(spec, spec),
        check_vma=False,
    )
```

```python
import jax
import jax.numpy as jnp
import numpy as np
from jax import lax
from jax.experimental import pallas as pl
from jax.experimental.pallas import tpu as pltpu
from jax.sharding import Mesh, PartitionSpec as P

FINE = ("zl2", "zl", "x1", "x0", "zh", "y", "c")
FINE_SIZES = (2, 4, 2, 2, 2, 8, 2)
E1 = ("zh", "zl2", "zl", "x1", "x0")
E2 = ("zl", "x1", "x0", "y", "c")
E3 = ("zh", "zl2", "x0", "y", "c")
BF = jnp.bfloat16
F32 = jnp.float32
NT = (((1,), (1,)), ((), ()))
NN = (((1,), (0,)), ((), ()))


def exchange(value, axes):
    return lax.all_to_all(value, axes, split_axis=0, concat_axis=0, tiled=True)


def parity_sign(value):
    for shift in (16, 8, 4, 2, 1):
        value = jnp.bitwise_xor(value, jnp.right_shift(value, shift))
    return (1 - 2 * jnp.bitwise_and(value, 1)).astype(F32)


def reorder(sizes, perm):
    source = np.arange(int(np.prod(sizes))).reshape(sizes).transpose(perm).reshape(-1)
    return (source[:, None] == np.arange(source.size)[None, :]).astype(np.float32)


VMEM = pl.BlockSpec(memory_space=pltpu.VMEM)
SMEM = pl.BlockSpec(memory_space=pltpu.SMEM)


def near(value):
    return pltpu.with_memory_space_constraint(value, pltpu.VMEM)


def dot(a, b, dims):
    return lax.dot_general(a, b, dims, preferred_element_type=F32)


def swap_pair(x0, x1, shift, lane):
    low = jnp.bitwise_and(lane, shift) == 0
    return (
        jnp.where(low, x0, pltpu.roll(x1, shift, 1)),
        jnp.where(low, pltpu.roll(x0, 128 - shift, 1), x1),
    )


def swap_quads(t, hi, lo, lane):
    a0, a2 = swap_pair(t[0], t[2], hi, lane)
    a1, a3 = swap_pair(t[1], t[3], hi, lane)
    b0, b1 = swap_pair(a0, a1, lo, lane)
    b2, b3 = swap_pair(a2, a3, lo, lane)
    return b0, b1, b2, b3


def lanes_of(rows):
    return lax.broadcasted_iota(jnp.int32, (rows, 128), 1)


def regroup(d_ref, q_ref, hi, lo):
    lane = lanes_of(32)
    for p in range(2):
        for g in range(4):
            t = [d_ref[pl.ds(p * 128 + i * 32, 32), pl.ds(g * 128, 128)] for i in range(4)]
            for s, block in enumerate(swap_quads(t, hi, lo, lane)):
                q_ref[pl.ds(g * 128 + s * 32, 32), pl.ds(p * 128, 128)] = block.astype(BF)


def pre_kernel(amp_ref, pr_ref, pc_ref, pm_ref, out_ref, z_ref):
    lane = lanes_of(32)
    for e in range(4):
        for p in range(2):
            turned = dot(pr_ref[...], amp_ref[p, e], NN).astype(BF)
            y = dot(pc_ref[...], turned, NT)
            t = [y[i * 32 : (i + 1) * 32] for i in range(4)]
            for i, block in enumerate(swap_quads(t, 64, 32, lane)):
                z_ref[pl.ds(p * 128 + i * 32, 32), pl.ds(e * 128, 128)] = block.astype(BF)
    moved = dot(pm_ref[...], z_ref[...], NN).astype(BF)
    for e in range(4):
        out_ref[pl.ds(e * 256, 256), :] = moved[:, e * 128 : (e + 1) * 128]


PR = reorder((32, 4), (1, 0))
PC = reorder((16, 2, 4), (2, 0, 1))
PM1 = reorder((2, 4, 16, 2), (2, 3, 0, 1))


def pre(amplitudes):
    out = pl.pallas_call(
        pre_kernel,
        in_specs=[VMEM] * 4,
        out_specs=VMEM,
        out_shape=pltpu.VMEM((1024, 128), BF),
        scratch_shapes=[pltpu.VMEM((256, 512), BF)],
        name="pre",
    )(amplitudes.reshape(2, 4, 128, 128), jnp.asarray(PR, BF), jnp.asarray(PC, BF), jnp.asarray(PM1, BF))
    return out.reshape(64, 16, 128)


def row_kernel(r_ref, v_ref, out_ref, x_ref, d_ref, q_ref):
    for b4 in range(2):
        x = r_ref[pl.ds(b4 * 512, 512), :].astype(F32).reshape(32, 2, 8, 128)
        for c1 in range(2):
            x_ref[:, pl.ds((b4 * 2 + c1) * 128, 128)] = x[:, c1].reshape(256, 128).astype(BF)
    d_ref[...] = dot(v_ref[0], x_ref[...], NN)
    regroup(d_ref, q_ref, 64, 32)
    d_ref[...] = dot(v_ref[1], q_ref[...], NT)
    regroup(d_ref, q_ref, 64, 32)
    d_ref[...] = dot(v_ref[2], q_ref[...], NT)
    regroup(d_ref, q_ref, 64, 32)
    d_ref[...] = dot(v_ref[3], q_ref[...], NT)
    lane = lanes_of(32)
    for piece in range(4):
        x = {}
        for p in range(2):
            for g in range(4):
                x[g >> 1, g & 1, p] = d_ref[pl.ds(p * 128 + piece * 32, 32), pl.ds(g * 128, 128)]
        for c1 in range(2):
            for p in range(2):
                x[0, c1, p], x[1, c1, p] = swap_pair(x[0, c1, p], x[1, c1, p], 8, lane)
        for b in range(2):
            for p in range(2):
                x[b, 0, p], x[b, 1, p] = swap_pair(x[b, 0, p], x[b, 1, p], 4, lane)
        for b in range(2):
            for c1 in range(2):
                x[b, c1, 0], x[b, c1, 1] = swap_pair(x[b, c1, 0], x[b, c1, 1], 2, lane)
        for (i, j, k), block in x.items():
            out_ref[pl.ds((i * 4 + j * 2 + k) * 128 + piece * 32, 32), :] = block.astype(BF)


def row_phase(r1, row):
    out = pl.pallas_call(
        row_kernel,
        in_specs=[VMEM] * 2,
        out_specs=VMEM,
        out_shape=pltpu.VMEM((1024, 128), BF),
        scratch_shapes=[pltpu.VMEM((256, 512), BF), pltpu.VMEM((256, 512), F32), pltpu.VMEM((512, 256), BF)],
        name="rows",
    )(near(r1.reshape(1024, 128)), near(row))
    return out.reshape(256, 4, 128)


def col_kernel(r_ref, v_ref, w_ref, s_ref, pm_ref, out_ref, d_ref, q_ref, f_ref, z_ref):
    lane = lanes_of(8)
    sub = lax.broadcasted_iota(jnp.int32, (8, 128), 0)
    high = jnp.bitwise_and(lane, 4) != 0
    keep = (jnp.bitwise_and(sub, 4) != 0) == high
    for kk in range(8):
        halves = []
        for k in (2 * kk, 2 * kk + 1):
            block = r_ref[pl.ds(k * 64, 64), :].astype(F32)
            x = {}
            for i in range(8):
                tile = block[i * 8 : (i + 1) * 8]
                turned = pltpu.roll(tile, 4, 0)
                other = jnp.where(high, pltpu.roll(turned, 4, 1), pltpu.roll(turned, 124, 1))
                x[i >> 2, (i >> 1) & 1, i & 1] = jnp.where(keep, tile, other)
            for i in range(2):
                for j in range(2):
                    x[0, i, j], x[1, i, j] = swap_pair(x[0, i, j], x[1, i, j], 16, lane)
            for i in range(2):
                for j in range(2):
                    x[i, 0, j], x[i, 1, j] = swap_pair(x[i, 0, j], x[i, 1, j], 2, lane)
            for i in range(2):
                for j in range(2):
                    x[i, j, 0], x[i, j, 1] = swap_pair(x[i, j, 0], x[i, j, 1], 1, lane)
            halves.append(x)
        for a4 in range(2):
            for p in range(2):
                for a0 in range(2):
                    both = jnp.concatenate([h[a4, p, a0] for h in halves], 0).astype(BF)
                    q_ref[pl.ds((a4 * 2 + a0) * 128 + kk * 16, 16), pl.ds(p * 128, 128)] = both
    d_ref[...] = dot(v_ref[0], q_ref[...], NT)
    regroup(d_ref, q_ref, 2, 1)
    d_ref[...] = dot(v_ref[1], q_ref[...], NT)
    regroup(d_ref, q_ref, 64, 32)
    d_ref[...] = dot(v_ref[2], q_ref[...], NT)
    regroup(d_ref, q_ref, 64, 32)
    state = dot(q_ref[...], v_ref[3], NN).astype(BF)
    f_ref[...] = state
    for g in range(4):
        for p in range(2):
            z_ref[pl.ds(p * 128, 128), pl.ds(g * 128, 128)] = f_ref[pl.ds(g * 128, 128), pl.ds(p * 128, 128)]
    moved = dot(pm_ref[...], z_ref[...], NN).astype(F32)
    for b4 in range(2):
        for g in range(4):
            part = moved[b4 * 128 : (b4 + 1) * 128, g * 128 : (g + 1) * 128].reshape(16, 8, 128)
            out_ref[b4, g, :, 0] = part.astype(BF)
    rows = f_ref[...].astype(F32)
    flips = (
        jnp.concatenate([rows[256:], rows[:256]], 0),
        swap_rows(rows, 16),
        swap_rows(rows, 128),
        swap_rows(rows, 8),
    )
    image = None
    for k in range(4):
        signed = (flips[k] * jnp.concatenate([s_ref[k], s_ref[k]], 1).astype(F32)).astype(BF)
        term = dot(signed, w_ref[k], NT)
        image = term if image is None else image + term
    image = image.astype(BF)
    for g in range(4):
        for p in range(2):
            z_ref[pl.ds(p * 128, 128), pl.ds(g * 128, 128)] = image[g * 128 : (g + 1) * 128, p * 128 : (p + 1) * 128]
    moved = dot(pm_ref[...], z_ref[...], NN)
    for b4 in range(2):
        for g in range(4):
            part = moved[b4 * 128 : (b4 + 1) * 128, g * 128 : (g + 1) * 128].reshape(16, 8, 128)
            out_ref[b4, g, :, 1] = part.astype(BF)


def swap_rows(rows, half):
    n = rows.shape[0] // (2 * half)
    r = rows.reshape(n, 2, half, rows.shape[1])
    return jnp.concatenate([r[:, 1:], r[:, :1]], 1).reshape(rows.shape)


PM2 = reorder((2, 4, 2, 2, 8), (2, 4, 3, 0, 1))


def col_phase(r2, col, image, signs):
    out = pl.pallas_call(
        col_kernel,
        in_specs=[VMEM] * 5,
        out_specs=VMEM,
        out_shape=pltpu.VMEM((2, 4, 16, 2, 8, 128), BF),
        scratch_shapes=[
            pltpu.VMEM((256, 512), F32),
            pltpu.VMEM((512, 256), BF),
            pltpu.VMEM((512, 256), BF),
            pltpu.VMEM((256, 512), BF),
        ],
        name="cols",
    )(near(r2.reshape(1024, 128)), near(col), near(image), near(signs), near(jnp.asarray(PM2, BF)))
    return out.reshape(128, 16, 128)


def post_kernel(r_ref, pm_ref, f_ref, i_ref):
    for e in range(4):
        x = r_ref[pl.ds(e * 512, 512), :].astype(F32).reshape(32, 2, 8, 128)
        x = jnp.concatenate([x[:, h].reshape(256, 128) for h in range(2)], 1).astype(BF)
        moved = dot(pm_ref[...], x, NN)
        for p in range(2):
            f_ref[p, e] = moved[p * 128 : (p + 1) * 128, :128].astype(BF)
            i_ref[p, e] = moved[p * 128 : (p + 1) * 128, 128:]


PM3 = reorder((32, 2, 4), (1, 0, 2))


def post(r3):
    f, i = pl.pallas_call(
        post_kernel,
        out_shape=(jax.ShapeDtypeStruct((2, 4, 128, 128), BF), jax.ShapeDtypeStruct((2, 4, 128, 128), F32)),
        in_specs=[VMEM] * 2,
        name="post",
    )(near(r3.reshape(2048, 128)), near(jnp.asarray(PM3, BF)))
    return f.reshape(2, 1, 1, 4, 128, 128), i.reshape(2, 1, 1, 4, 128, 128)


PT = reorder((2, 32, 4), (0, 2, 1))
C1 = reorder((2, 32, 4), (1, 0, 2))
C0 = reorder((2, 2, 2, 2, 2, 2, 4), (0, 6, 2, 1, 5, 3, 4))
R4 = reorder((2, 2, 8, 2, 4), (0, 4, 1, 3, 2))


def prep_kernel(flip_ref, mask_ref, mid_ref, g_ref, b_ref, p_ref, row_ref, col_ref, image_ref, sign_ref):
    pt = p_ref[0]

    def whole(real, imag):
        return jnp.concatenate(
            [jnp.concatenate([real, -imag], 1), jnp.concatenate([imag, real], 1)], 0
        )

    def moved(idx, left, right):
        v = whole(g_ref[idx, 0], g_ref[idx, 1])
        if left is not None:
            v = dot(left, v, NN).astype(BF)
        if right is not None:
            v = dot(v, right, NT).astype(BF)
        return v

    row_ref[0] = moved(1, pt, p_ref[1])
    row_ref[1] = moved(3, pt, pt)
    row_ref[2] = moved(5, pt, pt)
    row_ref[3] = moved(7, None, pt)
    col_ref[0] = moved(0, pt, p_ref[2])
    col_ref[1] = moved(2, pt, None)
    col_ref[2] = moved(4, p_ref[3], pt)
    col_ref[3] = dot(pt, whole(g_ref[6, 0], g_ref[6, 1]), NT).astype(BF)
    out_col = lax.broadcasted_iota(jnp.int32, (128, 128), 0)
    in_col = lax.broadcasted_iota(jnp.int32, (128, 128), 1)
    spot = lax.broadcasted_iota(jnp.int32, (512, 128), 0)
    o = jnp.bitwise_and(spot, 31)
    b = jnp.bitwise_and(o, 16) + jnp.bitwise_and(o, 7) * 2 + jnp.bitwise_and(jnp.right_shift(o, 3), 1)
    a = jnp.right_shift(spot, 8) * 16 + jnp.bitwise_and(jnp.right_shift(spot, 7), 1) + mid_ref[0]
    index = (a * 32 + b) * 128
    for k in range(4):
        onehot = (out_col == jnp.bitwise_xor(in_col, flip_ref[k])).astype(F32).astype(BF)
        sign = parity_sign(jnp.bitwise_and(out_col, mask_ref[k]))
        parts = [(dot(b_ref[k, q], onehot, NN) * sign).astype(BF) for q in range(2)]
        image_ref[k] = whole(parts[0], parts[1])
        sign_ref[k] = parity_sign(jnp.bitwise_and(index, mask_ref[k])).astype(BF)


def prep(gates, blocks, flips, masks, a_mid):
    square = pltpu.VMEM((4, 256, 256), BF)
    return pl.pallas_call(
        prep_kernel,
        in_specs=[SMEM] * 3 + [VMEM] * 3,
        out_specs=(VMEM,) * 4,
        out_shape=(square, square, square, pltpu.VMEM((4, 512, 128), BF)),
        name="prep",
    )(flips, masks, a_mid.reshape(1).astype(jnp.int32), gates, blocks, jnp.asarray(np.stack([PT, C1, C0, R4]), BF))


def local(amplitudes, layer_gates, pauli_blocks, flip_masks, phase_masks):
    a_mid = lax.axis_index("zl") * 4 + lax.axis_index("x1") * 2
    row, col, image, signs = prep(layer_gates, pauli_blocks, flip_masks, phase_masks, a_mid)
    r1 = exchange(pre(amplitudes), E1)
    r2 = exchange(row_phase(r1, row), E2)
    r3 = exchange(col_phase(r2, col, image, signs), E3)
    return post(r3)


def solution(mesh):
    fine = Mesh(mesh.devices.reshape(FINE_SIZES), FINE)
    spec = P(None, ("zl2", "zl", "x1", "x0"), ("zh", "y", "c"), None, None, None)
    return jax.shard_map(
        local,
        mesh=fine,
        in_specs=(spec, P(), P(), P(), P()),
        out_specs=(spec, spec),
        check_vma=False,
    )
```

```python
import jax
import jax.numpy as jnp
import numpy as np
from jax import lax
from jax.experimental import pallas as pl
from jax.experimental.pallas import tpu as pltpu
from jax.sharding import Mesh, PartitionSpec as P

FINE = ("zl2", "zl", "x1", "x0", "zh", "y", "c")
FINE_SIZES = (2, 4, 2, 2, 2, 8, 2)
E1 = ("zh", "zl2", "zl", "x1", "x0")
E2 = ("zl", "x1", "x0", "y", "c")
E3 = ("zh", "zl2", "x0", "y", "c")
BF = jnp.bfloat16
F32 = jnp.float32
NT = (((1,), (1,)), ((), ()))
NN = (((1,), (0,)), ((), ()))


def exchange(value, axes):
    return lax.all_to_all(value, axes, split_axis=0, concat_axis=0, tiled=True)


def parity_sign(value):
    for shift in (16, 8, 4, 2, 1):
        value = jnp.bitwise_xor(value, jnp.right_shift(value, shift))
    return (1 - 2 * jnp.bitwise_and(value, 1)).astype(F32)


def reorder(sizes, perm):
    source = np.arange(int(np.prod(sizes))).reshape(sizes).transpose(perm).reshape(-1)
    return (source[:, None] == np.arange(source.size)[None, :]).astype(np.float32)


VMEM = pl.BlockSpec(memory_space=pltpu.VMEM)
ANY = pl.BlockSpec(memory_space=pl.ANY)
SMEM = pl.BlockSpec(memory_space=pltpu.SMEM)


def near(value):
    return pltpu.with_memory_space_constraint(value, pltpu.VMEM)


def dot(a, b, dims):
    return lax.dot_general(a, b, dims, preferred_element_type=F32)


def swap_pair(x0, x1, shift, lane):
    low = jnp.bitwise_and(lane, shift) == 0
    return (
        jnp.where(low, x0, pltpu.roll(x1, shift, 1)),
        jnp.where(low, pltpu.roll(x0, 128 - shift, 1), x1),
    )


def swap_quads(t, hi, lo, lane):
    a0, a2 = swap_pair(t[0], t[2], hi, lane)
    a1, a3 = swap_pair(t[1], t[3], hi, lane)
    b0, b1 = swap_pair(a0, a1, lo, lane)
    b2, b3 = swap_pair(a2, a3, lo, lane)
    return b0, b1, b2, b3


def lanes_of(rows):
    return lax.broadcasted_iota(jnp.int32, (rows, 128), 1)


def regroup(d_ref, q_ref, hi, lo):
    lane = lanes_of(32)
    for p in range(2):
        for g in range(4):
            t = [d_ref[pl.ds(p * 128 + i * 32, 32), pl.ds(g * 128, 128)] for i in range(4)]
            for s, block in enumerate(swap_quads(t, hi, lo, lane)):
                q_ref[pl.ds(g * 128 + s * 32, 32), pl.ds(p * 128, 128)] = block


def pre_kernel(amp_ref, pr_ref, pc_ref, pm_ref, out_ref, in_v, pr_v, pc_v, pm_v, z_ref, out_v, in_sem, const_sem, out_sem):
    loads = [pltpu.make_async_copy(amp_ref.at[:, e], in_v.at[:, e], in_sem.at[e]) for e in range(4)]
    consts = [
        pltpu.make_async_copy(src, dst, const_sem.at[i])
        for i, (src, dst) in enumerate(((pr_ref, pr_v), (pc_ref, pc_v), (pm_ref, pm_v)))
    ]
    consts[0].start()
    loads[0].start()
    consts[1].start()
    consts[2].start()
    for e in range(1, 4):
        loads[e].start()
    lane = lanes_of(32)
    stores = []
    for e in range(4):
        if e == 0:
            consts[0].wait()
            consts[1].wait()
        loads[e].wait()
        for p in range(2):
            turned = dot(pr_v[...], in_v[p, e], NN).astype(BF)
            y = dot(pc_v[...], turned, NT)
            t = [y[i * 32 : (i + 1) * 32] for i in range(4)]
            for i, block in enumerate(swap_quads(t, 64, 32, lane)):
                z_ref[e, pl.ds(p * 128 + i * 32, 32), :] = block.astype(BF)
        if e == 0:
            consts[2].wait()
        out_v[e] = dot(pm_v[...], z_ref[e], NN).astype(BF)
        store = pltpu.make_async_copy(out_v.at[e], out_ref.at[pl.ds(e * 256, 256)], out_sem.at[e])
        store.start()
        stores.append(store)
    for store in stores:
        store.wait()


PR = reorder((32, 4), (1, 0))
PC = reorder((16, 2, 4), (2, 0, 1))
PM1 = reorder((2, 4, 16, 2), (2, 3, 0, 1))


def pre(amplitudes):
    out = pl.pallas_call(
        pre_kernel,
        in_specs=[ANY] * 4,
        out_specs=ANY,
        out_shape=jax.ShapeDtypeStruct((1024, 128), BF),
        scratch_shapes=[
            pltpu.VMEM((2, 4, 128, 128), BF),
            pltpu.VMEM((128, 128), BF),
            pltpu.VMEM((128, 128), BF),
            pltpu.VMEM((256, 256), BF),
            pltpu.VMEM((4, 256, 128), BF),
            pltpu.VMEM((4, 256, 128), BF),
            pltpu.SemaphoreType.DMA((4,)),
            pltpu.SemaphoreType.DMA((3,)),
            pltpu.SemaphoreType.DMA((4,)),
        ],
        name="pre",
    )(amplitudes.reshape(2, 4, 128, 128), jnp.asarray(PR, BF), jnp.asarray(PC, BF), jnp.asarray(PM1, BF))
    return out.reshape(64, 16, 128)


def row_kernel(r_ref, v_ref, out_ref, x_ref, d_ref, q_ref):
    for b4 in range(2):
        x = r_ref[pl.ds(b4 * 512, 512), :].astype(F32).reshape(32, 2, 8, 128)
        for c1 in range(2):
            x_ref[:, pl.ds((b4 * 2 + c1) * 128, 128)] = x[:, c1].reshape(256, 128).astype(BF)
    d_ref[...] = dot(v_ref[0], x_ref[...], NN).astype(BF)
    regroup(d_ref, q_ref, 64, 32)
    d_ref[...] = dot(v_ref[1], q_ref[...], NT).astype(BF)
    regroup(d_ref, q_ref, 64, 32)
    d_ref[...] = dot(v_ref[2], q_ref[...], NT).astype(BF)
    regroup(d_ref, q_ref, 64, 32)
    d_ref[...] = dot(v_ref[3], q_ref[...], NT).astype(BF)
    lane = lanes_of(32)
    for piece in range(4):
        x = {}
        for p in range(2):
            for g in range(4):
                x[g >> 1, g & 1, p] = d_ref[pl.ds(p * 128 + piece * 32, 32), pl.ds(g * 128, 128)]
        for c1 in range(2):
            for p in range(2):
                x[0, c1, p], x[1, c1, p] = swap_pair(x[0, c1, p], x[1, c1, p], 8, lane)
        for b in range(2):
            for p in range(2):
                x[b, 0, p], x[b, 1, p] = swap_pair(x[b, 0, p], x[b, 1, p], 4, lane)
        for b in range(2):
            for c1 in range(2):
                x[b, c1, 0], x[b, c1, 1] = swap_pair(x[b, c1, 0], x[b, c1, 1], 2, lane)
        for (i, j, k), block in x.items():
            out_ref[pl.ds((i * 4 + j * 2 + k) * 128 + piece * 32, 32), :] = block


def row_phase(r1, row):
    out = pl.pallas_call(
        row_kernel,
        in_specs=[VMEM] * 2,
        out_specs=VMEM,
        out_shape=pltpu.VMEM((1024, 128), BF),
        scratch_shapes=[pltpu.VMEM((256, 512), BF), pltpu.VMEM((256, 512), BF), pltpu.VMEM((512, 256), BF)],
        name="rows",
    )(near(r1.reshape(1024, 128)), near(row))
    return out.reshape(256, 4, 128)


def col_kernel(r_ref, v_ref, w_ref, s_ref, pm_ref, out_ref, d_ref, q_ref, f_ref, z_ref):
    lane = lanes_of(8)
    sub = lax.broadcasted_iota(jnp.int32, (8, 128), 0)
    high = jnp.bitwise_and(lane, 4) != 0
    keep = (jnp.bitwise_and(sub, 4) != 0) == high
    for kk in range(8):
        halves = []
        for k in (2 * kk, 2 * kk + 1):
            block = r_ref[pl.ds(k * 64, 64), :].astype(F32)
            x = {}
            for i in range(8):
                tile = block[i * 8 : (i + 1) * 8]
                turned = pltpu.roll(tile, 4, 0)
                other = jnp.where(high, pltpu.roll(turned, 4, 1), pltpu.roll(turned, 124, 1))
                x[i >> 2, (i >> 1) & 1, i & 1] = jnp.where(keep, tile, other)
            for i in range(2):
                for j in range(2):
                    x[0, i, j], x[1, i, j] = swap_pair(x[0, i, j], x[1, i, j], 16, lane)
            for i in range(2):
                for j in range(2):
                    x[i, 0, j], x[i, 1, j] = swap_pair(x[i, 0, j], x[i, 1, j], 2, lane)
            for i in range(2):
                for j in range(2):
                    x[i, j, 0], x[i, j, 1] = swap_pair(x[i, j, 0], x[i, j, 1], 1, lane)
            halves.append(x)
        for a4 in range(2):
            for p in range(2):
                for a0 in range(2):
                    both = jnp.concatenate([h[a4, p, a0] for h in halves], 0).astype(BF)
                    q_ref[pl.ds((a4 * 2 + a0) * 128 + kk * 16, 16), pl.ds(p * 128, 128)] = both
    d_ref[...] = dot(v_ref[0], q_ref[...], NT).astype(BF)
    regroup(d_ref, q_ref, 2, 1)
    d_ref[...] = dot(v_ref[1], q_ref[...], NT).astype(BF)
    regroup(d_ref, q_ref, 64, 32)
    d_ref[...] = dot(v_ref[2], q_ref[...], NT).astype(BF)
    regroup(d_ref, q_ref, 64, 32)
    state = dot(q_ref[...], v_ref[3], NN).astype(BF)
    f_ref[...] = state
    for g in range(4):
        for p in range(2):
            z_ref[pl.ds(p * 128, 128), pl.ds(g * 128, 128)] = f_ref[pl.ds(g * 128, 128), pl.ds(p * 128, 128)]
    moved = dot(pm_ref[...], z_ref[...], NN).astype(F32)
    for b4 in range(2):
        for g in range(4):
            part = moved[b4 * 128 : (b4 + 1) * 128, g * 128 : (g + 1) * 128].reshape(16, 8, 128)
            out_ref[b4, g, :, 0] = part.astype(BF)
    rows = f_ref[...].astype(F32)
    flips = (
        jnp.concatenate([rows[256:], rows[:256]], 0),
        swap_rows(rows, 16),
        swap_rows(rows, 128),
        swap_rows(rows, 8),
    )
    image = None
    for k in range(4):
        signed = (flips[k] * jnp.concatenate([s_ref[k], s_ref[k]], 1).astype(F32)).astype(BF)
        term = dot(signed, w_ref[k], NT)
        image = term if image is None else image + term
    image = image.astype(BF)
    for g in range(4):
        for p in range(2):
            z_ref[pl.ds(p * 128, 128), pl.ds(g * 128, 128)] = image[g * 128 : (g + 1) * 128, p * 128 : (p + 1) * 128]
    moved = dot(pm_ref[...], z_ref[...], NN)
    for b4 in range(2):
        for g in range(4):
            part = moved[b4 * 128 : (b4 + 1) * 128, g * 128 : (g + 1) * 128].reshape(16, 8, 128)
            out_ref[b4, g, :, 1] = part.astype(BF)


def swap_rows(rows, half):
    n = rows.shape[0] // (2 * half)
    r = rows.reshape(n, 2, half, rows.shape[1])
    return jnp.concatenate([r[:, 1:], r[:, :1]], 1).reshape(rows.shape)


PM2 = reorder((2, 4, 2, 2, 8), (2, 4, 3, 0, 1))


def col_phase(r2, col, image, signs):
    out = pl.pallas_call(
        col_kernel,
        in_specs=[VMEM] * 5,
        out_specs=VMEM,
        out_shape=pltpu.VMEM((2, 4, 16, 2, 8, 128), BF),
        scratch_shapes=[
            pltpu.VMEM((256, 512), BF),
            pltpu.VMEM((512, 256), BF),
            pltpu.VMEM((512, 256), BF),
            pltpu.VMEM((256, 512), BF),
        ],
        name="cols",
    )(near(r2.reshape(1024, 128)), near(col), near(image), near(signs), near(jnp.asarray(PM2, BF)))
    return out.reshape(128, 16, 128)


def post_kernel(r_ref, pm_ref, f_ref, i_ref):
    for e in range(4):
        x = r_ref[pl.ds(e * 512, 512), :].astype(F32).reshape(32, 2, 8, 128)
        x = jnp.concatenate([x[:, h].reshape(256, 128) for h in range(2)], 1).astype(BF)
        moved = dot(pm_ref[...], x, NN)
        for p in range(2):
            f_ref[p, e] = moved[p * 128 : (p + 1) * 128, :128].astype(BF)
            i_ref[p, e] = moved[p * 128 : (p + 1) * 128, 128:]


PM3 = reorder((32, 2, 4), (1, 0, 2))


def post(r3):
    f, i = pl.pallas_call(
        post_kernel,
        out_shape=(jax.ShapeDtypeStruct((2, 4, 128, 128), BF), jax.ShapeDtypeStruct((2, 4, 128, 128), F32)),
        in_specs=[VMEM] * 2,
        name="post",
    )(near(r3.reshape(2048, 128)), near(jnp.asarray(PM3, BF)))
    return f.reshape(2, 1, 1, 4, 128, 128), i.reshape(2, 1, 1, 4, 128, 128)


PT = reorder((2, 32, 4), (0, 2, 1))
C1 = reorder((2, 32, 4), (1, 0, 2))
C0 = reorder((2, 2, 2, 2, 2, 2, 4), (0, 6, 2, 1, 5, 3, 4))
R4 = reorder((2, 2, 8, 2, 4), (0, 4, 1, 3, 2))


def prep_kernel(flip_ref, mask_ref, mid_ref, g_ref, b_ref, p_ref, row_ref, col_ref, image_ref, sign_ref):
    pt = p_ref[0]

    def whole(real, imag):
        return jnp.concatenate(
            [jnp.concatenate([real, -imag], 1), jnp.concatenate([imag, real], 1)], 0
        )

    def moved(idx, left, right):
        v = whole(g_ref[idx, 0], g_ref[idx, 1])
        if left is not None:
            v = dot(left, v, NN).astype(BF)
        if right is not None:
            v = dot(v, right, NT).astype(BF)
        return v

    row_ref[0] = moved(1, pt, p_ref[1])
    row_ref[1] = moved(3, pt, pt)
    row_ref[2] = moved(5, pt, pt)
    row_ref[3] = moved(7, None, pt)
    col_ref[0] = moved(0, pt, p_ref[2])
    col_ref[1] = moved(2, pt, None)
    col_ref[2] = moved(4, p_ref[3], pt)
    col_ref[3] = dot(pt, whole(g_ref[6, 0], g_ref[6, 1]), NT).astype(BF)
    out_col = lax.broadcasted_iota(jnp.int32, (128, 128), 0)
    in_col = lax.broadcasted_iota(jnp.int32, (128, 128), 1)
    spot = lax.broadcasted_iota(jnp.int32, (512, 128), 0)
    o = jnp.bitwise_and(spot, 31)
    b = jnp.bitwise_and(o, 16) + jnp.bitwise_and(o, 7) * 2 + jnp.bitwise_and(jnp.right_shift(o, 3), 1)
    a = jnp.right_shift(spot, 8) * 16 + jnp.bitwise_and(jnp.right_shift(spot, 7), 1) + mid_ref[0]
    index = (a * 32 + b) * 128
    for k in range(4):
        onehot = (out_col == jnp.bitwise_xor(in_col, flip_ref[k])).astype(F32).astype(BF)
        sign = parity_sign(jnp.bitwise_and(out_col, mask_ref[k]))
        parts = [(dot(b_ref[k, q], onehot, NN) * sign).astype(BF) for q in range(2)]
        image_ref[k] = whole(parts[0], parts[1])
        sign_ref[k] = parity_sign(jnp.bitwise_and(index, mask_ref[k])).astype(BF)


def prep(gates, blocks, flips, masks, a_mid):
    square = pltpu.VMEM((4, 256, 256), BF)
    return pl.pallas_call(
        prep_kernel,
        in_specs=[SMEM] * 3 + [VMEM] * 3,
        out_specs=(VMEM,) * 4,
        out_shape=(square, square, square, pltpu.VMEM((4, 512, 128), BF)),
        name="prep",
    )(flips, masks, a_mid.reshape(1).astype(jnp.int32), gates, blocks, jnp.asarray(np.stack([PT, C1, C0, R4]), BF))


def local(amplitudes, layer_gates, pauli_blocks, flip_masks, phase_masks):
    a_mid = lax.axis_index("zl") * 4 + lax.axis_index("x1") * 2
    row, col, image, signs = prep(layer_gates, pauli_blocks, flip_masks, phase_masks, a_mid)
    r1 = exchange(pre(amplitudes), E1)
    r2 = exchange(row_phase(r1, row), E2)
    r3 = exchange(col_phase(r2, col, image, signs), E3)
    return post(r3)


def solution(mesh):
    fine = Mesh(mesh.devices.reshape(FINE_SIZES), FINE)
    spec = P(None, ("zl2", "zl", "x1", "x0"), ("zh", "y", "c"), None, None, None)
    return jax.shard_map(
        local,
        mesh=fine,
        in_specs=(spec, P(), P(), P(), P()),
        out_specs=(spec, spec),
        check_vma=False,
    )
```

```python
import jax
import jax.numpy as jnp
import numpy as np
from jax import lax
from jax.experimental import pallas as pl
from jax.experimental.pallas import tpu as pltpu
from jax.sharding import Mesh, PartitionSpec as P

FINE = ("zl2", "zl", "x1", "x0", "zh", "y", "c")
FINE_SIZES = (2, 4, 2, 2, 2, 8, 2)
E1 = ("zh", "zl2", "zl", "x1", "x0")
E2 = ("c", "zl", "x1", "x0", "y")
E3 = ("zh", "zl2", "x0", "y", "c")
BF = jnp.bfloat16
F32 = jnp.float32
NT = (((1,), (1,)), ((), ()))
NN = (((1,), (0,)), ((), ()))


def exchange(value, axes):
    return lax.all_to_all(value, axes, split_axis=0, concat_axis=0, tiled=True)


def parity_sign(value):
    for shift in (16, 8, 4, 2, 1):
        value = jnp.bitwise_xor(value, jnp.right_shift(value, shift))
    return (1 - 2 * jnp.bitwise_and(value, 1)).astype(F32)


def reorder(sizes, perm):
    source = np.arange(int(np.prod(sizes))).reshape(sizes).transpose(perm).reshape(-1)
    return (source[:, None] == np.arange(source.size)[None, :]).astype(np.float32)


VMEM = pl.BlockSpec(memory_space=pltpu.VMEM)
SMEM = pl.BlockSpec(memory_space=pltpu.SMEM)


def near(value):
    return pltpu.with_memory_space_constraint(value, pltpu.VMEM)


def dot(a, b, dims):
    return lax.dot_general(a, b, dims, preferred_element_type=F32)


def swap_pair(x0, x1, shift, lane):
    low = jnp.bitwise_and(lane, shift) == 0
    return (
        jnp.where(low, x0, pltpu.roll(x1, shift, 1)),
        jnp.where(low, pltpu.roll(x0, 128 - shift, 1), x1),
    )


def swap_quads(t, hi, lo, lane):
    a0, a2 = swap_pair(t[0], t[2], hi, lane)
    a1, a3 = swap_pair(t[1], t[3], hi, lane)
    b0, b1 = swap_pair(a0, a1, lo, lane)
    b2, b3 = swap_pair(a2, a3, lo, lane)
    return b0, b1, b2, b3


def lanes_of(rows):
    return lax.broadcasted_iota(jnp.int32, (rows, 128), 1)


def regroup(d_ref, q_ref, hi, lo):
    lane = lanes_of(32)
    for p in range(2):
        for g in range(4):
            t = [d_ref[pl.ds(p * 128 + i * 32, 32), pl.ds(g * 128, 128)] for i in range(4)]
            for s, block in enumerate(swap_quads(t, hi, lo, lane)):
                q_ref[pl.ds(g * 128 + s * 32, 32), pl.ds(p * 128, 128)] = block.astype(BF)


def pre_kernel(amp_ref, pr_ref, pc_ref, pm_ref, out_ref, z_ref):
    lane = lanes_of(32)
    for e in range(4):
        for p in range(2):
            turned = dot(pr_ref[...], amp_ref[p, e], NN).astype(BF)
            y = dot(pc_ref[...], turned, NT)
            t = [y[i * 32 : (i + 1) * 32] for i in range(4)]
            for i, block in enumerate(swap_quads(t, 64, 32, lane)):
                z_ref[pl.ds(p * 128 + i * 32, 32), pl.ds(e * 128, 128)] = block.astype(BF)
    moved = dot(pm_ref[...], z_ref[...], NN).astype(BF)
    for e in range(4):
        out_ref[pl.ds(e * 256, 256), :] = moved[:, e * 128 : (e + 1) * 128]


PR = reorder((32, 4), (1, 0))
PC = reorder((16, 2, 4), (2, 0, 1))
PM1 = reorder((2, 4, 16, 2), (2, 3, 0, 1))


def pre(amplitudes):
    out = pl.pallas_call(
        pre_kernel,
        in_specs=[VMEM] * 4,
        out_specs=VMEM,
        out_shape=pltpu.VMEM((1024, 128), BF),
        scratch_shapes=[pltpu.VMEM((256, 512), BF)],
        name="pre",
    )(amplitudes.reshape(2, 4, 128, 128), jnp.asarray(PR, BF), jnp.asarray(PC, BF), jnp.asarray(PM1, BF))
    return out.reshape(64, 16, 128)


def row_kernel(r_ref, v_ref, out_ref, x_ref, d_ref, q_ref):
    for b4 in range(2):
        x = r_ref[pl.ds(b4 * 512, 512), :].astype(F32).reshape(32, 2, 8, 128)
        for c1 in range(2):
            x_ref[:, pl.ds((b4 * 2 + c1) * 128, 128)] = x[:, c1].reshape(256, 128).astype(BF)
    d_ref[...] = dot(v_ref[0], x_ref[...], NN)
    regroup(d_ref, q_ref, 64, 32)
    d_ref[...] = dot(v_ref[1], q_ref[...], NT)
    regroup(d_ref, q_ref, 64, 32)
    d_ref[...] = dot(v_ref[2], q_ref[...], NT)
    regroup(d_ref, q_ref, 64, 32)
    d_ref[...] = dot(v_ref[3], q_ref[...], NT)
    lane = lanes_of(32)
    for piece in range(4):
        x = {}
        for p in range(2):
            for g in range(4):
                x[g >> 1, g & 1, p] = d_ref[pl.ds(p * 128 + piece * 32, 32), pl.ds(g * 128, 128)]
        for c1 in range(2):
            for p in range(2):
                x[0, c1, p], x[1, c1, p] = swap_pair(x[0, c1, p], x[1, c1, p], 8, lane)
        for b in range(2):
            for p in range(2):
                x[b, 0, p], x[b, 1, p] = swap_pair(x[b, 0, p], x[b, 1, p], 4, lane)
        for b in range(2):
            for c1 in range(2):
                x[b, c1, 0], x[b, c1, 1] = swap_pair(x[b, c1, 0], x[b, c1, 1], 2, lane)
        for (i, j, k), block in x.items():
            spot = (piece >> 1) * 512 + (i * 4 + j * 2 + k) * 64 + (piece & 1) * 32
            out_ref[pl.ds(spot, 32), :] = block.astype(BF)


def row_phase(r1, row):
    out = pl.pallas_call(
        row_kernel,
        in_specs=[VMEM] * 2,
        out_specs=VMEM,
        out_shape=pltpu.VMEM((1024, 128), BF),
        scratch_shapes=[pltpu.VMEM((256, 512), BF), pltpu.VMEM((256, 512), F32), pltpu.VMEM((512, 256), BF)],
        name="rows",
    )(near(r1.reshape(1024, 128)), near(row))
    return out.reshape(256, 4, 128)


def col_kernel(r_ref, v_ref, w_ref, s_ref, pm_ref, out_ref, d_ref, q_ref, f_ref, z_ref):
    lane = lanes_of(8)
    sub = lax.broadcasted_iota(jnp.int32, (8, 128), 0)
    high = jnp.bitwise_and(lane, 4) != 0
    keep = (jnp.bitwise_and(sub, 4) != 0) == high
    for kk in range(8):
        halves = []
        for k in (2 * kk, 2 * kk + 1):
            blocks = [r_ref[pl.ds(c * 512 + k * 32, 32), :].astype(F32) for c in range(2)]
            x = {}
            for i in range(8):
                tile = blocks[i & 1][(i >> 1) * 8 : (i >> 1) * 8 + 8]
                turned = pltpu.roll(tile, 4, 0)
                other = jnp.where(high, pltpu.roll(turned, 4, 1), pltpu.roll(turned, 124, 1))
                x[i >> 2, (i >> 1) & 1, i & 1] = jnp.where(keep, tile, other)
            for i in range(2):
                for j in range(2):
                    x[0, i, j], x[1, i, j] = swap_pair(x[0, i, j], x[1, i, j], 16, lane)
            for i in range(2):
                for j in range(2):
                    x[i, 0, j], x[i, 1, j] = swap_pair(x[i, 0, j], x[i, 1, j], 2, lane)
            for i in range(2):
                for j in range(2):
                    x[i, j, 0], x[i, j, 1] = swap_pair(x[i, j, 0], x[i, j, 1], 1, lane)
            halves.append(x)
        for a4 in range(2):
            for p in range(2):
                for a0 in range(2):
                    both = jnp.concatenate([h[a4, p, a0] for h in halves], 0).astype(BF)
                    q_ref[pl.ds((a4 * 2 + a0) * 128 + kk * 16, 16), pl.ds(p * 128, 128)] = both
    d_ref[...] = dot(v_ref[0], q_ref[...], NT)
    regroup(d_ref, q_ref, 2, 1)
    d_ref[...] = dot(v_ref[1], q_ref[...], NT)
    regroup(d_ref, q_ref, 64, 32)
    d_ref[...] = dot(v_ref[2], q_ref[...], NT)
    regroup(d_ref, q_ref, 64, 32)
    state = dot(q_ref[...], v_ref[3], NN).astype(BF)
    f_ref[...] = state
    for g in range(4):
        for p in range(2):
            z_ref[pl.ds(p * 128, 128), pl.ds(g * 128, 128)] = f_ref[pl.ds(g * 128, 128), pl.ds(p * 128, 128)]
    moved = dot(pm_ref[...], z_ref[...], NN).astype(F32)
    for b4 in range(2):
        for g in range(4):
            part = moved[b4 * 128 : (b4 + 1) * 128, g * 128 : (g + 1) * 128].reshape(16, 8, 128)
            out_ref[b4, g, :, 0] = part.astype(BF)
    rows = f_ref[...].astype(F32)
    flips = (
        jnp.concatenate([rows[256:], rows[:256]], 0),
        swap_rows(rows, 16),
        swap_rows(rows, 128),
        swap_rows(rows, 8),
    )
    image = None
    for k in range(4):
        signed = (flips[k] * jnp.concatenate([s_ref[k], s_ref[k]], 1).astype(F32)).astype(BF)
        term = dot(signed, w_ref[k], NT)
        image = term if image is None else image + term
    image = image.astype(BF)
    for g in range(4):
        for p in range(2):
            z_ref[pl.ds(p * 128, 128), pl.ds(g * 128, 128)] = image[g * 128 : (g + 1) * 128, p * 128 : (p + 1) * 128]
    moved = dot(pm_ref[...], z_ref[...], NN)
    for b4 in range(2):
        for g in range(4):
            part = moved[b4 * 128 : (b4 + 1) * 128, g * 128 : (g + 1) * 128].reshape(16, 8, 128)
            out_ref[b4, g, :, 1] = part.astype(BF)


def swap_rows(rows, half):
    n = rows.shape[0] // (2 * half)
    r = rows.reshape(n, 2, half, rows.shape[1])
    return jnp.concatenate([r[:, 1:], r[:, :1]], 1).reshape(rows.shape)


PM2 = reorder((2, 4, 2, 2, 8), (2, 4, 3, 0, 1))


def col_phase(r2, col, image, signs):
    out = pl.pallas_call(
        col_kernel,
        in_specs=[VMEM] * 5,
        out_specs=VMEM,
        out_shape=pltpu.VMEM((2, 4, 16, 2, 8, 128), BF),
        scratch_shapes=[
            pltpu.VMEM((256, 512), F32),
            pltpu.VMEM((512, 256), BF),
            pltpu.VMEM((512, 256), BF),
            pltpu.VMEM((256, 512), BF),
        ],
        name="cols",
    )(near(r2.reshape(1024, 128)), near(col), near(image), near(signs), near(jnp.asarray(PM2, BF)))
    return out.reshape(128, 16, 128)


def post_kernel(r_ref, pm_ref, f_ref, i_ref):
    for e in range(4):
        x = r_ref[pl.ds(e * 512, 512), :].astype(F32).reshape(32, 2, 8, 128)
        x = jnp.concatenate([x[:, h].reshape(256, 128) for h in range(2)], 1).astype(BF)
        moved = dot(pm_ref[...], x, NN)
        for p in range(2):
            f_ref[p, e] = moved[p * 128 : (p + 1) * 128, :128].astype(BF)
            i_ref[p, e] = moved[p * 128 : (p + 1) * 128, 128:]


PM3 = reorder((32, 2, 4), (1, 0, 2))


def post(r3):
    f, i = pl.pallas_call(
        post_kernel,
        out_shape=(jax.ShapeDtypeStruct((2, 4, 128, 128), BF), jax.ShapeDtypeStruct((2, 4, 128, 128), F32)),
        in_specs=[VMEM] * 2,
        name="post",
    )(near(r3.reshape(2048, 128)), near(jnp.asarray(PM3, BF)))
    return f.reshape(2, 1, 1, 4, 128, 128), i.reshape(2, 1, 1, 4, 128, 128)


PT = reorder((2, 32, 4), (0, 2, 1))
C1 = reorder((2, 32, 4), (1, 0, 2))
C0 = reorder((2, 2, 2, 2, 2, 2, 4), (0, 6, 2, 1, 4, 3, 5))
R7 = reorder((2, 16, 2, 4), (0, 2, 1, 3))
R4 = reorder((2, 2, 8, 2, 4), (0, 4, 1, 3, 2))


def prep_kernel(flip_ref, mask_ref, mid_ref, g_ref, b_ref, p_ref, row_ref, col_ref, image_ref, sign_ref):
    pt = p_ref[0]

    def whole(real, imag):
        return jnp.concatenate(
            [jnp.concatenate([real, -imag], 1), jnp.concatenate([imag, real], 1)], 0
        )

    def moved(idx, left, right):
        v = whole(g_ref[idx, 0], g_ref[idx, 1])
        if left is not None:
            v = dot(left, v, NN).astype(BF)
        if right is not None:
            v = dot(v, right, NT).astype(BF)
        return v

    row_ref[0] = moved(1, pt, p_ref[1])
    row_ref[1] = moved(3, pt, pt)
    row_ref[2] = moved(5, pt, pt)
    row_ref[3] = moved(7, p_ref[4], pt)
    col_ref[0] = moved(0, pt, p_ref[2])
    col_ref[1] = moved(2, pt, None)
    col_ref[2] = moved(4, p_ref[3], pt)
    col_ref[3] = dot(pt, whole(g_ref[6, 0], g_ref[6, 1]), NT).astype(BF)
    out_col = lax.broadcasted_iota(jnp.int32, (128, 128), 0)
    in_col = lax.broadcasted_iota(jnp.int32, (128, 128), 1)
    spot = lax.broadcasted_iota(jnp.int32, (512, 128), 0)
    o = jnp.bitwise_and(spot, 31)
    b = jnp.bitwise_and(o, 16) + jnp.bitwise_and(o, 7) * 2 + jnp.bitwise_and(jnp.right_shift(o, 3), 1)
    a = jnp.right_shift(spot, 8) * 16 + jnp.bitwise_and(jnp.right_shift(spot, 7), 1) + mid_ref[0]
    index = (a * 32 + b) * 128
    for k in range(4):
        onehot = (out_col == jnp.bitwise_xor(in_col, flip_ref[k])).astype(F32).astype(BF)
        sign = parity_sign(jnp.bitwise_and(out_col, mask_ref[k]))
        parts = [(dot(b_ref[k, q], onehot, NN) * sign).astype(BF) for q in range(2)]
        image_ref[k] = whole(parts[0], parts[1])
        sign_ref[k] = parity_sign(jnp.bitwise_and(index, mask_ref[k])).astype(BF)


def prep(gates, blocks, flips, masks, a_mid):
    square = pltpu.VMEM((4, 256, 256), BF)
    return pl.pallas_call(
        prep_kernel,
        in_specs=[SMEM] * 3 + [VMEM] * 3,
        out_specs=(VMEM,) * 4,
        out_shape=(square, square, square, pltpu.VMEM((4, 512, 128), BF)),
        name="prep",
    )(flips, masks, a_mid.reshape(1).astype(jnp.int32), gates, blocks, jnp.asarray(np.stack([PT, C1, C0, R4, R7]), BF))


def local(amplitudes, layer_gates, pauli_blocks, flip_masks, phase_masks):
    a_mid = lax.axis_index("zl") * 4 + lax.axis_index("x1") * 2
    row, col, image, signs = prep(layer_gates, pauli_blocks, flip_masks, phase_masks, a_mid)
    r1 = exchange(pre(amplitudes), E1)
    r2 = exchange(row_phase(r1, row), E2)
    r3 = exchange(col_phase(r2, col, image, signs), E3)
    return post(r3)


def solution(mesh):
    fine = Mesh(mesh.devices.reshape(FINE_SIZES), FINE)
    spec = P(None, ("zl2", "zl", "x1", "x0"), ("zh", "y", "c"), None, None, None)
    return jax.shard_map(
        local,
        mesh=fine,
        in_specs=(spec, P(), P(), P(), P()),
        out_specs=(spec, spec),
        check_vma=False,
    )
```

```python
import jax
import jax.numpy as jnp
import numpy as np
from jax import lax
from jax.experimental import pallas as pl
from jax.experimental.pallas import tpu as pltpu
from jax.sharding import Mesh, PartitionSpec as P

FINE = ("zl2", "zl", "x1", "x0", "zh", "y", "c")
FINE_SIZES = (2, 4, 2, 2, 2, 8, 2)
E1 = ("zh", "zl2", "zl", "x1", "x0")
E2 = ("c", "zl", "x1", "x0", "y")
E3 = ("zh", "zl2", "x0", "y", "c")
BF = jnp.bfloat16
F32 = jnp.float32
NT = (((1,), (1,)), ((), ()))
NN = (((1,), (0,)), ((), ()))


def exchange(value, axes):
    return lax.all_to_all(value, axes, split_axis=0, concat_axis=0, tiled=True)


def parity_sign(value):
    for shift in (16, 8, 4, 2, 1):
        value = jnp.bitwise_xor(value, jnp.right_shift(value, shift))
    return (1 - 2 * jnp.bitwise_and(value, 1)).astype(F32)


def reorder(sizes, perm):
    source = np.arange(int(np.prod(sizes))).reshape(sizes).transpose(perm).reshape(-1)
    return (source[:, None] == np.arange(source.size)[None, :]).astype(np.float32)


VMEM = pl.BlockSpec(memory_space=pltpu.VMEM)
ANY = pl.BlockSpec(memory_space=pl.ANY)
SMEM = pl.BlockSpec(memory_space=pltpu.SMEM)


def near(value):
    return pltpu.with_memory_space_constraint(value, pltpu.VMEM)


def dot(a, b, dims):
    return lax.dot_general(a, b, dims, preferred_element_type=F32)


def swap_pair(x0, x1, shift, lane):
    low = jnp.bitwise_and(lane, shift) == 0
    return (
        jnp.where(low, x0, pltpu.roll(x1, shift, 1)),
        jnp.where(low, pltpu.roll(x0, 128 - shift, 1), x1),
    )


def swap_quads(t, hi, lo, lane):
    a0, a2 = swap_pair(t[0], t[2], hi, lane)
    a1, a3 = swap_pair(t[1], t[3], hi, lane)
    b0, b1 = swap_pair(a0, a1, lo, lane)
    b2, b3 = swap_pair(a2, a3, lo, lane)
    return b0, b1, b2, b3


def lanes_of(rows):
    return lax.broadcasted_iota(jnp.int32, (rows, 128), 1)


def regroup(d_ref, q_ref, hi, lo):
    lane = lanes_of(32)
    for p in range(2):
        for g in range(4):
            t = [d_ref[pl.ds(p * 128 + i * 32, 32), pl.ds(g * 128, 128)] for i in range(4)]
            for s, block in enumerate(swap_quads(t, hi, lo, lane)):
                q_ref[pl.ds(g * 128 + s * 32, 32), pl.ds(p * 128, 128)] = block.astype(BF)


def picks(size, source_of):
    row = lax.broadcasted_iota(jnp.int32, (size, 128), 0)
    col = lax.broadcasted_iota(jnp.int32, (size, 128), 1)
    source = source_of(row)
    parts = [(source == col + off).astype(F32) for off in range(0, size, 128)]
    return (jnp.concatenate(parts, 1) if len(parts) > 1 else parts[0]).astype(BF)


def pre_kernel(amp_hbm, out_ref, amp_ref, pr_ref, pc_ref, pm_ref, z_ref, sem):
    load = pltpu.make_async_copy(amp_hbm, amp_ref, sem)
    load.start()
    pr_ref[...] = picks(128, lambda r: (r & 31) * 4 + (r >> 5))
    pc_ref[...] = picks(128, lambda r: ((r >> 1) & 15) * 8 + (r & 1) * 4 + (r >> 5))
    pm_ref[...] = picks(256, lambda r: ((r >> 2) & 1) * 128 + (r & 3) * 32 + (r >> 4) * 2 + ((r >> 3) & 1))
    load.wait()
    lane = lanes_of(32)
    for e in range(4):
        for p in range(2):
            turned = dot(pr_ref[...], amp_ref[p, e], NN).astype(BF)
            y = dot(pc_ref[...], turned, NT)
            t = [y[i * 32 : (i + 1) * 32] for i in range(4)]
            for i, block in enumerate(swap_quads(t, 64, 32, lane)):
                z_ref[pl.ds(p * 128 + i * 32, 32), pl.ds(e * 128, 128)] = block.astype(BF)
    moved = dot(pm_ref[...], z_ref[...], NN).astype(BF)
    for e in range(4):
        out_ref[pl.ds(e * 256, 256), :] = moved[:, e * 128 : (e + 1) * 128]


def pre(amplitudes):
    out = pl.pallas_call(
        pre_kernel,
        in_specs=[ANY],
        out_specs=VMEM,
        out_shape=pltpu.VMEM((1024, 128), BF),
        scratch_shapes=[
            pltpu.VMEM((2, 4, 128, 128), BF),
            pltpu.VMEM((128, 128), BF),
            pltpu.VMEM((128, 128), BF),
            pltpu.VMEM((256, 256), BF),
            pltpu.VMEM((256, 512), BF),
            pltpu.SemaphoreType.DMA,
        ],
        name="pre",
    )(amplitudes.reshape(2, 4, 128, 128))
    return out.reshape(64, 16, 128)


def row_kernel(r_ref, v_ref, out_ref, x_ref, d_ref, q_ref):
    for b4 in range(2):
        x = r_ref[pl.ds(b4 * 512, 512), :].astype(F32).reshape(32, 2, 8, 128)
        for c1 in range(2):
            x_ref[:, pl.ds((b4 * 2 + c1) * 128, 128)] = x[:, c1].reshape(256, 128).astype(BF)
    d_ref[...] = dot(v_ref[0], x_ref[...], NN)
    regroup(d_ref, q_ref, 64, 32)
    d_ref[...] = dot(v_ref[1], q_ref[...], NT)
    regroup(d_ref, q_ref, 64, 32)
    d_ref[...] = dot(v_ref[2], q_ref[...], NT)
    regroup(d_ref, q_ref, 64, 32)
    d_ref[...] = dot(v_ref[3], q_ref[...], NT)
    lane = lanes_of(32)
    for piece in range(4):
        x = {}
        for p in range(2):
            for g in range(4):
                x[g >> 1, g & 1, p] = d_ref[pl.ds(p * 128 + piece * 32, 32), pl.ds(g * 128, 128)]
        for c1 in range(2):
            for p in range(2):
                x[0, c1, p], x[1, c1, p] = swap_pair(x[0, c1, p], x[1, c1, p], 8, lane)
        for b in range(2):
            for p in range(2):
                x[b, 0, p], x[b, 1, p] = swap_pair(x[b, 0, p], x[b, 1, p], 4, lane)
        for b in range(2):
            for c1 in range(2):
                x[b, c1, 0], x[b, c1, 1] = swap_pair(x[b, c1, 0], x[b, c1, 1], 2, lane)
        for (i, j, k), block in x.items():
            spot = (piece >> 1) * 512 + (i * 4 + j * 2 + k) * 64 + (piece & 1) * 32
            out_ref[pl.ds(spot, 32), :] = block.astype(BF)


def row_phase(r1, row):
    out = pl.pallas_call(
        row_kernel,
        in_specs=[VMEM] * 2,
        out_specs=VMEM,
        out_shape=pltpu.VMEM((1024, 128), BF),
        scratch_shapes=[pltpu.VMEM((256, 512), BF), pltpu.VMEM((256, 512), F32), pltpu.VMEM((512, 256), BF)],
        name="rows",
    )(near(r1.reshape(1024, 128)), near(row))
    return out.reshape(256, 4, 128)


def col_kernel(r_ref, v_ref, w_ref, s_ref, pm_ref, out_ref, d_ref, q_ref, f_ref, z_ref, g_ref):
    lane = lanes_of(8)
    sub = lax.broadcasted_iota(jnp.int32, (8, 128), 0)
    high = jnp.bitwise_and(lane, 4) != 0
    keep = (jnp.bitwise_and(sub, 4) != 0) == high
    for kk in range(8):
        halves = []
        for k in (2 * kk, 2 * kk + 1):
            blocks = [r_ref[pl.ds(c * 512 + k * 32, 32), :].astype(F32) for c in range(2)]
            x = {}
            for i in range(8):
                tile = blocks[i & 1][(i >> 1) * 8 : (i >> 1) * 8 + 8]
                turned = pltpu.roll(tile, 4, 0)
                other = jnp.where(high, pltpu.roll(turned, 4, 1), pltpu.roll(turned, 124, 1))
                x[i >> 2, (i >> 1) & 1, i & 1] = jnp.where(keep, tile, other)
            for i in range(2):
                for j in range(2):
                    x[0, i, j], x[1, i, j] = swap_pair(x[0, i, j], x[1, i, j], 16, lane)
            for i in range(2):
                for j in range(2):
                    x[i, 0, j], x[i, 1, j] = swap_pair(x[i, 0, j], x[i, 1, j], 2, lane)
            for i in range(2):
                for j in range(2):
                    x[i, j, 0], x[i, j, 1] = swap_pair(x[i, j, 0], x[i, j, 1], 1, lane)
            halves.append(x)
        for a4 in range(2):
            for p in range(2):
                for a0 in range(2):
                    both = jnp.concatenate([h[a4, p, a0] for h in halves], 0).astype(BF)
                    q_ref[pl.ds((a4 * 2 + a0) * 128 + kk * 16, 16), pl.ds(p * 128, 128)] = both
    d_ref[...] = dot(v_ref[0], q_ref[...], NT)
    regroup(d_ref, q_ref, 2, 1)
    d_ref[...] = dot(v_ref[1], q_ref[...], NT)
    regroup(d_ref, q_ref, 64, 32)
    d_ref[...] = dot(v_ref[2], q_ref[...], NT)
    regroup(d_ref, q_ref, 64, 32)
    state = dot(q_ref[...], v_ref[3], NN).astype(BF)
    f_ref[...] = state
    for g in range(4):
        for p in range(2):
            z_ref[pl.ds(p * 128, 128), pl.ds(g * 128, 128)] = f_ref[pl.ds(g * 128, 128), pl.ds(p * 128, 128)]
    moved = dot(pm_ref[...], z_ref[...], NN).astype(F32)
    for b4 in range(2):
        for g in range(4):
            part = moved[b4 * 128 : (b4 + 1) * 128, g * 128 : (g + 1) * 128].reshape(16, 8, 128)
            out_ref[b4, g, :, 0] = part.astype(BF)
    for k in range(4):
        for r in range(0, 512, 32):
            source = r ^ (256, 0, 128, 0)[k]
            for p in range(2):
                half = pl.ds(p * 128, 128)
                if k == 1:
                    block = jnp.concatenate([f_ref[pl.ds(r + 16, 16), half], f_ref[pl.ds(r, 16), half]], 0)
                elif k == 3:
                    wide = f_ref[pl.ds(r, 32), half].astype(F32)
                    block = jnp.concatenate([wide[8:16], wide[:8], wide[24:], wide[16:24]], 0).astype(BF)
                else:
                    block = f_ref[pl.ds(source, 32), half]
                g_ref[pl.ds(r, 32), pl.ds(k * 256 + p * 128, 128)] = block * s_ref[k, pl.ds(r, 32), :]
    image = dot(g_ref[...], w_ref[...], NT)
    image = image.astype(BF)
    for g in range(4):
        for p in range(2):
            z_ref[pl.ds(p * 128, 128), pl.ds(g * 128, 128)] = image[g * 128 : (g + 1) * 128, p * 128 : (p + 1) * 128]
    moved = dot(pm_ref[...], z_ref[...], NN)
    for b4 in range(2):
        for g in range(4):
            part = moved[b4 * 128 : (b4 + 1) * 128, g * 128 : (g + 1) * 128].reshape(16, 8, 128)
            out_ref[b4, g, :, 1] = part.astype(BF)


PM2 = reorder((2, 4, 2, 2, 8), (2, 4, 3, 0, 1))


def col_phase(r2, col, image, signs):
    out = pl.pallas_call(
        col_kernel,
        in_specs=[VMEM] * 5,
        out_specs=VMEM,
        out_shape=pltpu.VMEM((2, 4, 16, 2, 8, 128), BF),
        scratch_shapes=[
            pltpu.VMEM((256, 512), F32),
            pltpu.VMEM((512, 256), BF),
            pltpu.VMEM((512, 256), BF),
            pltpu.VMEM((256, 512), BF),
            pltpu.VMEM((512, 1024), BF),
        ],
        name="cols",
    )(near(r2.reshape(1024, 128)), near(col), near(image), near(signs), near(jnp.asarray(PM2, BF)))
    return out.reshape(128, 16, 128)


def post_kernel(r_ref, pm_ref, f_ref, i_ref):
    for e in range(4):
        x = r_ref[pl.ds(e * 512, 512), :].astype(F32).reshape(32, 2, 8, 128)
        x = jnp.concatenate([x[:, h].reshape(256, 128) for h in range(2)], 1).astype(BF)
        moved = dot(pm_ref[...], x, NN)
        for p in range(2):
            f_ref[p, e] = moved[p * 128 : (p + 1) * 128, :128].astype(BF)
            i_ref[p, e] = moved[p * 128 : (p + 1) * 128, 128:]


PM3 = reorder((32, 2, 4), (1, 0, 2))


def post(r3):
    f, i = pl.pallas_call(
        post_kernel,
        out_shape=(jax.ShapeDtypeStruct((2, 4, 128, 128), BF), jax.ShapeDtypeStruct((2, 4, 128, 128), F32)),
        in_specs=[VMEM] * 2,
        name="post",
    )(near(r3.reshape(2048, 128)), near(jnp.asarray(PM3, BF)))
    return f.reshape(2, 1, 1, 4, 128, 128), i.reshape(2, 1, 1, 4, 128, 128)


PT = reorder((2, 32, 4), (0, 2, 1))
C1 = reorder((2, 32, 4), (1, 0, 2))
C0 = reorder((2, 2, 2, 2, 2, 2, 4), (0, 6, 2, 1, 4, 3, 5))
R7 = reorder((2, 16, 2, 4), (0, 2, 1, 3))
R4 = reorder((2, 2, 8, 2, 4), (0, 4, 1, 3, 2))


def prep_kernel(flip_ref, mask_ref, mid_ref, g_ref, b_ref, p_ref, row_ref, col_ref, image_ref, sign_ref):
    pt = p_ref[0]

    def whole(real, imag):
        return jnp.concatenate(
            [jnp.concatenate([real, -imag], 1), jnp.concatenate([imag, real], 1)], 0
        )

    def moved(idx, left, right):
        v = whole(g_ref[idx, 0], g_ref[idx, 1])
        if left is not None:
            v = dot(left, v, NN).astype(BF)
        if right is not None:
            v = dot(v, right, NT).astype(BF)
        return v

    row_ref[0] = moved(1, pt, p_ref[1])
    row_ref[1] = moved(3, pt, pt)
    row_ref[2] = moved(5, pt, pt)
    row_ref[3] = moved(7, p_ref[4], pt)
    col_ref[0] = moved(0, pt, p_ref[2])
    col_ref[1] = moved(2, pt, None)
    col_ref[2] = moved(4, p_ref[3], pt)
    col_ref[3] = dot(pt, whole(g_ref[6, 0], g_ref[6, 1]), NT).astype(BF)
    out_col = lax.broadcasted_iota(jnp.int32, (128, 128), 0)
    in_col = lax.broadcasted_iota(jnp.int32, (128, 128), 1)
    spot = lax.broadcasted_iota(jnp.int32, (512, 128), 0)
    o = jnp.bitwise_and(spot, 31)
    b = jnp.bitwise_and(o, 16) + jnp.bitwise_and(o, 7) * 2 + jnp.bitwise_and(jnp.right_shift(o, 3), 1)
    a = jnp.right_shift(spot, 8) * 16 + jnp.bitwise_and(jnp.right_shift(spot, 7), 1) + mid_ref[0]
    index = (a * 32 + b) * 128
    for k in range(4):
        onehot = (out_col == jnp.bitwise_xor(in_col, flip_ref[k])).astype(F32).astype(BF)
        sign = parity_sign(jnp.bitwise_and(out_col, mask_ref[k]))
        parts = [(dot(b_ref[k, q], onehot, NN) * sign).astype(BF) for q in range(2)]
        image_ref[:, pl.ds(k * 256, 256)] = whole(parts[0], parts[1])
        sign_ref[k] = parity_sign(jnp.bitwise_and(index, mask_ref[k])).astype(BF)


def prep(gates, blocks, flips, masks, a_mid):
    square = pltpu.VMEM((4, 256, 256), BF)
    return pl.pallas_call(
        prep_kernel,
        in_specs=[SMEM] * 3 + [VMEM] * 3,
        out_specs=(VMEM,) * 4,
        out_shape=(square, square, pltpu.VMEM((256, 1024), BF), pltpu.VMEM((4, 512, 128), BF)),
        name="prep",
    )(flips, masks, a_mid.reshape(1).astype(jnp.int32), gates, blocks, jnp.asarray(np.stack([PT, C1, C0, R4, R7]), BF))


def local(amplitudes, layer_gates, pauli_blocks, flip_masks, phase_masks):
    a_mid = lax.axis_index("zl") * 4 + lax.axis_index("x1") * 2
    row, col, image, signs = prep(layer_gates, pauli_blocks, flip_masks, phase_masks, a_mid)
    r1 = exchange(pre(amplitudes), E1)
    r2 = exchange(row_phase(r1, row), E2)
    r3 = exchange(col_phase(r2, col, image, signs), E3)
    return post(r3)


def solution(mesh):
    fine = Mesh(mesh.devices.reshape(FINE_SIZES), FINE)
    spec = P(None, ("zl2", "zl", "x1", "x0"), ("zh", "y", "c"), None, None, None)
    return jax.shard_map(
        local,
        mesh=fine,
        in_specs=(spec, P(), P(), P(), P()),
        out_specs=(spec, spec),
        check_vma=False,
    )
```

```python
import jax
import jax.numpy as jnp
import numpy as np
from jax import lax
from jax.experimental import pallas as pl
from jax.experimental.pallas import tpu as pltpu
from jax.sharding import Mesh, PartitionSpec as P

FINE = ("zl2", "zl", "x1", "x0", "zh", "y", "c")
FINE_SIZES = (2, 4, 2, 2, 2, 8, 2)
E1 = ("zh", "zl2", "zl", "x1", "x0")
E2 = ("c", "zl", "x1", "x0", "y")
E3 = ("c", "x0", "zh", "zl2", "y")
BF = jnp.bfloat16
F32 = jnp.float32
NT = (((1,), (1,)), ((), ()))
NN = (((1,), (0,)), ((), ()))


def exchange(value, axes):
    return lax.all_to_all(value, axes, split_axis=0, concat_axis=0, tiled=True)


def parity_sign(value):
    for shift in (16, 8, 4, 2, 1):
        value = jnp.bitwise_xor(value, jnp.right_shift(value, shift))
    return (1 - 2 * jnp.bitwise_and(value, 1)).astype(F32)


def reorder(sizes, perm):
    source = np.arange(int(np.prod(sizes))).reshape(sizes).transpose(perm).reshape(-1)
    return (source[:, None] == np.arange(source.size)[None, :]).astype(np.float32)


VMEM = pl.BlockSpec(memory_space=pltpu.VMEM)
SMEM = pl.BlockSpec(memory_space=pltpu.SMEM)


def near(value):
    return pltpu.with_memory_space_constraint(value, pltpu.VMEM)


def dot(a, b, dims):
    return lax.dot_general(a, b, dims, preferred_element_type=F32)


def swap_pair(x0, x1, shift, lane):
    low = jnp.bitwise_and(lane, shift) == 0
    return (
        jnp.where(low, x0, pltpu.roll(x1, shift, 1)),
        jnp.where(low, pltpu.roll(x0, 128 - shift, 1), x1),
    )


def swap_quads(t, hi, lo, lane):
    a0, a2 = swap_pair(t[0], t[2], hi, lane)
    a1, a3 = swap_pair(t[1], t[3], hi, lane)
    b0, b1 = swap_pair(a0, a1, lo, lane)
    b2, b3 = swap_pair(a2, a3, lo, lane)
    return b0, b1, b2, b3


def lanes_of(rows):
    return lax.broadcasted_iota(jnp.int32, (rows, 128), 1)


def regroup(d_ref, q_ref, hi, lo):
    lane = lanes_of(32)
    for p in range(2):
        for g in range(4):
            t = [d_ref[pl.ds(p * 128 + i * 32, 32), pl.ds(g * 128, 128)] for i in range(4)]
            for s, block in enumerate(swap_quads(t, hi, lo, lane)):
                q_ref[pl.ds(g * 128 + s * 32, 32), pl.ds(p * 128, 128)] = block.astype(BF)


def pre_kernel(amp_ref, pr_ref, pc_ref, pm_ref, out_ref, z_ref):
    lane = lanes_of(32)
    for e in range(4):
        for p in range(2):
            turned = dot(pr_ref[...], amp_ref[p, e], NN).astype(BF)
            y = dot(pc_ref[...], turned, NT)
            t = [y[i * 32 : (i + 1) * 32] for i in range(4)]
            for i, block in enumerate(swap_quads(t, 64, 32, lane)):
                z_ref[pl.ds(p * 128 + i * 32, 32), pl.ds(e * 128, 128)] = block.astype(BF)
    moved = dot(pm_ref[...], z_ref[...], NN).astype(BF)
    for e in range(4):
        out_ref[pl.ds(e * 256, 256), :] = moved[:, e * 128 : (e + 1) * 128]


PR = reorder((32, 4), (1, 0))
PC = reorder((16, 2, 4), (2, 0, 1))
PM1 = reorder((2, 4, 16, 2), (2, 3, 0, 1))


def pre(amplitudes):
    out = pl.pallas_call(
        pre_kernel,
        in_specs=[VMEM] * 4,
        out_specs=VMEM,
        out_shape=pltpu.VMEM((1024, 128), BF),
        scratch_shapes=[pltpu.VMEM((256, 512), BF)],
        name="pre",
    )(amplitudes.reshape(2, 4, 128, 128), jnp.asarray(PR, BF), jnp.asarray(PC, BF), jnp.asarray(PM1, BF))
    return out.reshape(64, 16, 128)


def row_kernel(r_ref, v_ref, out_ref, x_ref, d_ref, q_ref):
    for b4 in range(2):
        x = r_ref[pl.ds(b4 * 512, 512), :].astype(F32).reshape(32, 2, 8, 128)
        for c1 in range(2):
            x_ref[:, pl.ds((b4 * 2 + c1) * 128, 128)] = x[:, c1].reshape(256, 128).astype(BF)
    d_ref[...] = dot(v_ref[0], x_ref[...], NN)
    regroup(d_ref, q_ref, 64, 32)
    d_ref[...] = dot(v_ref[1], q_ref[...], NT)
    regroup(d_ref, q_ref, 64, 32)
    d_ref[...] = dot(v_ref[2], q_ref[...], NT)
    regroup(d_ref, q_ref, 64, 32)
    d_ref[...] = dot(v_ref[3], q_ref[...], NT)
    lane = lanes_of(32)
    for piece in range(4):
        x = {}
        for p in range(2):
            for g in range(4):
                x[g >> 1, g & 1, p] = d_ref[pl.ds(p * 128 + piece * 32, 32), pl.ds(g * 128, 128)]
        for c1 in range(2):
            for p in range(2):
                x[0, c1, p], x[1, c1, p] = swap_pair(x[0, c1, p], x[1, c1, p], 8, lane)
        for b in range(2):
            for p in range(2):
                x[b, 0, p], x[b, 1, p] = swap_pair(x[b, 0, p], x[b, 1, p], 4, lane)
        for b in range(2):
            for c1 in range(2):
                x[b, c1, 0], x[b, c1, 1] = swap_pair(x[b, c1, 0], x[b, c1, 1], 2, lane)
        for (i, j, k), block in x.items():
            spot = (piece >> 1) * 512 + (i * 4 + j * 2 + k) * 64 + (piece & 1) * 32
            out_ref[pl.ds(spot, 32), :] = block.astype(BF)


def row_phase(r1, row):
    out = pl.pallas_call(
        row_kernel,
        in_specs=[VMEM] * 2,
        out_specs=VMEM,
        out_shape=pltpu.VMEM((1024, 128), BF),
        scratch_shapes=[pltpu.VMEM((256, 512), BF), pltpu.VMEM((256, 512), F32), pltpu.VMEM((512, 256), BF)],
        name="rows",
    )(near(r1.reshape(1024, 128)), near(row))
    return out.reshape(256, 4, 128)


def col_kernel(r_ref, v_ref, w_ref, s_ref, pm_ref, out_ref, d_ref, q_ref, f_ref, z_ref):
    lane = lanes_of(8)
    sub = lax.broadcasted_iota(jnp.int32, (8, 128), 0)
    high = jnp.bitwise_and(lane, 4) != 0
    keep = (jnp.bitwise_and(sub, 4) != 0) == high
    for kk in range(8):
        halves = []
        for k in (2 * kk, 2 * kk + 1):
            blocks = [r_ref[pl.ds(c * 512 + k * 32, 32), :].astype(F32) for c in range(2)]
            x = {}
            for i in range(8):
                tile = blocks[i & 1][(i >> 1) * 8 : (i >> 1) * 8 + 8]
                turned = pltpu.roll(tile, 4, 0)
                other = jnp.where(high, pltpu.roll(turned, 4, 1), pltpu.roll(turned, 124, 1))
                x[i >> 2, (i >> 1) & 1, i & 1] = jnp.where(keep, tile, other)
            for i in range(2):
                for j in range(2):
                    x[0, i, j], x[1, i, j] = swap_pair(x[0, i, j], x[1, i, j], 16, lane)
            for i in range(2):
                for j in range(2):
                    x[i, 0, j], x[i, 1, j] = swap_pair(x[i, 0, j], x[i, 1, j], 2, lane)
            for i in range(2):
                for j in range(2):
                    x[i, j, 0], x[i, j, 1] = swap_pair(x[i, j, 0], x[i, j, 1], 1, lane)
            halves.append(x)
        for a4 in range(2):
            for p in range(2):
                for a0 in range(2):
                    both = jnp.concatenate([h[a4, p, a0] for h in halves], 0).astype(BF)
                    q_ref[pl.ds((a4 * 2 + a0) * 128 + kk * 16, 16), pl.ds(p * 128, 128)] = both
    d_ref[...] = dot(v_ref[0], q_ref[...], NT)
    regroup(d_ref, q_ref, 2, 1)
    d_ref[...] = dot(v_ref[1], q_ref[...], NT)
    regroup(d_ref, q_ref, 64, 32)
    d_ref[...] = dot(v_ref[2], q_ref[...], NT)
    regroup(d_ref, q_ref, 64, 32)
    state = dot(q_ref[...], v_ref[3], NN).astype(BF)
    f_ref[...] = state
    for g in range(4):
        for p in range(2):
            z_ref[pl.ds(p * 128, 128), pl.ds(g * 128, 128)] = f_ref[pl.ds(g * 128, 128), pl.ds(p * 128, 128)]
    moved = dot(pm_ref[...], z_ref[...], NN).astype(F32)
    for b in range(4):
        for g in range(4):
            part = moved[b * 64 : (b + 1) * 64, g * 128 : (g + 1) * 128].reshape(8, 8, 128)
            out_ref[b & 1, g & 1, b >> 1, g >> 1, :, 0] = part.astype(BF)
    rows = f_ref[...].astype(F32)
    flips = (
        jnp.concatenate([rows[256:], rows[:256]], 0),
        swap_rows(rows, 16),
        swap_rows(rows, 128),
        swap_rows(rows, 8),
    )
    image = None
    for k in range(4):
        signed = (flips[k] * jnp.concatenate([s_ref[k], s_ref[k]], 1).astype(F32)).astype(BF)
        term = dot(signed, w_ref[k], NT)
        image = term if image is None else image + term
    image = image.astype(BF)
    for g in range(4):
        for p in range(2):
            z_ref[pl.ds(p * 128, 128), pl.ds(g * 128, 128)] = image[g * 128 : (g + 1) * 128, p * 128 : (p + 1) * 128]
    moved = dot(pm_ref[...], z_ref[...], NN)
    for b in range(4):
        for g in range(4):
            part = moved[b * 64 : (b + 1) * 64, g * 128 : (g + 1) * 128].reshape(8, 8, 128)
            out_ref[b & 1, g & 1, b >> 1, g >> 1, :, 1] = part.astype(BF)


def swap_rows(rows, half):
    n = rows.shape[0] // (2 * half)
    r = rows.reshape(n, 2, half, rows.shape[1])
    return jnp.concatenate([r[:, 1:], r[:, :1]], 1).reshape(rows.shape)


PM2 = reorder((2, 4, 2, 2, 8), (2, 3, 4, 0, 1))


def col_phase(r2, col, image, signs):
    out = pl.pallas_call(
        col_kernel,
        in_specs=[VMEM] * 5,
        out_specs=VMEM,
        out_shape=pltpu.VMEM((2, 2, 2, 2, 8, 2, 8, 128), BF),
        scratch_shapes=[
            pltpu.VMEM((256, 512), F32),
            pltpu.VMEM((512, 256), BF),
            pltpu.VMEM((512, 256), BF),
            pltpu.VMEM((256, 512), BF),
        ],
        name="cols",
    )(near(r2.reshape(1024, 128)), near(col), near(image), near(signs), near(jnp.asarray(PM2, BF)))
    return out.reshape(128, 16, 128)


def post_kernel(r_ref, pm_ref, f_ref, i_ref):
    for e in range(4):
        x = jnp.concatenate([r_ref[pl.ds(i * 512 + e * 128, 128), :] for i in range(4)], 0)
        x = x.astype(F32).reshape(32, 2, 8, 128)
        x = jnp.concatenate([x[:, h].reshape(256, 128) for h in range(2)], 1).astype(BF)
        moved = dot(pm_ref[...], x, NN)
        for p in range(2):
            f_ref[p, e] = moved[p * 128 : (p + 1) * 128, :128].astype(BF)
            i_ref[p, e] = moved[p * 128 : (p + 1) * 128, 128:]


PM3 = reorder((2, 2, 8, 2, 4), (3, 1, 2, 0, 4))


def post(r3):
    f, i = pl.pallas_call(
        post_kernel,
        out_shape=(jax.ShapeDtypeStruct((2, 4, 128, 128), BF), jax.ShapeDtypeStruct((2, 4, 128, 128), F32)),
        in_specs=[VMEM] * 2,
        name="post",
    )(near(r3.reshape(2048, 128)), near(jnp.asarray(PM3, BF)))
    return f.reshape(2, 1, 1, 4, 128, 128), i.reshape(2, 1, 1, 4, 128, 128)


PT = reorder((2, 32, 4), (0, 2, 1))
C1 = reorder((2, 32, 4), (1, 0, 2))
C0 = reorder((2, 2, 2, 2, 2, 2, 4), (0, 6, 2, 1, 4, 3, 5))
R7 = reorder((2, 16, 2, 4), (0, 2, 1, 3))
R4 = reorder((2, 2, 8, 2, 4), (0, 4, 1, 3, 2))


def prep_kernel(flip_ref, mask_ref, mid_ref, g_ref, b_ref, p_ref, row_ref, col_ref, image_ref, sign_ref):
    pt = p_ref[0]

    def whole(real, imag):
        return jnp.concatenate(
            [jnp.concatenate([real, -imag], 1), jnp.concatenate([imag, real], 1)], 0
        )

    def moved(idx, left, right):
        v = whole(g_ref[idx, 0], g_ref[idx, 1])
        if left is not None:
            v = dot(left, v, NN).astype(BF)
        if right is not None:
            v = dot(v, right, NT).astype(BF)
        return v

    row_ref[0] = moved(1, pt, p_ref[1])
    row_ref[1] = moved(3, pt, pt)
    row_ref[2] = moved(5, pt, pt)
    row_ref[3] = moved(7, p_ref[4], pt)
    col_ref[0] = moved(0, pt, p_ref[2])
    col_ref[1] = moved(2, pt, None)
    col_ref[2] = moved(4, p_ref[3], pt)
    col_ref[3] = dot(pt, whole(g_ref[6, 0], g_ref[6, 1]), NT).astype(BF)
    out_col = lax.broadcasted_iota(jnp.int32, (128, 128), 0)
    in_col = lax.broadcasted_iota(jnp.int32, (128, 128), 1)
    spot = lax.broadcasted_iota(jnp.int32, (512, 128), 0)
    o = jnp.bitwise_and(spot, 31)
    b = jnp.bitwise_and(o, 16) + jnp.bitwise_and(o, 7) * 2 + jnp.bitwise_and(jnp.right_shift(o, 3), 1)
    a = jnp.right_shift(spot, 8) * 16 + jnp.bitwise_and(jnp.right_shift(spot, 7), 1) + mid_ref[0]
    index = (a * 32 + b) * 128
    for k in range(4):
        onehot = (out_col == jnp.bitwise_xor(in_col, flip_ref[k])).astype(F32).astype(BF)
        sign = parity_sign(jnp.bitwise_and(out_col, mask_ref[k]))
        parts = [(dot(b_ref[k, q], onehot, NN) * sign).astype(BF) for q in range(2)]
        image_ref[k] = whole(parts[0], parts[1])
        sign_ref[k] = parity_sign(jnp.bitwise_and(index, mask_ref[k])).astype(BF)


def prep(gates, blocks, flips, masks, a_mid):
    square = pltpu.VMEM((4, 256, 256), BF)
    return pl.pallas_call(
        prep_kernel,
        in_specs=[SMEM] * 3 + [VMEM] * 3,
        out_specs=(VMEM,) * 4,
        out_shape=(square, square, square, pltpu.VMEM((4, 512, 128), BF)),
        name="prep",
    )(flips, masks, a_mid.reshape(1).astype(jnp.int32), gates, blocks, jnp.asarray(np.stack([PT, C1, C0, R4, R7]), BF))


def local(amplitudes, layer_gates, pauli_blocks, flip_masks, phase_masks):
    a_mid = lax.axis_index("zl") * 4 + lax.axis_index("x1") * 2
    row, col, image, signs = prep(layer_gates, pauli_blocks, flip_masks, phase_masks, a_mid)
    r1 = exchange(pre(amplitudes), E1)
    r2 = exchange(row_phase(r1, row), E2)
    r3 = exchange(col_phase(r2, col, image, signs), E3)
    return post(r3)


def solution(mesh):
    fine = Mesh(mesh.devices.reshape(FINE_SIZES), FINE)
    spec = P(None, ("zl2", "zl", "x1", "x0"), ("zh", "y", "c"), None, None, None)
    return jax.shard_map(
        local,
        mesh=fine,
        in_specs=(spec, P(), P(), P(), P()),
        out_specs=(spec, spec),
        check_vma=False,
    )
```
